32 devices in a mesh: ctx: 4 (over y, x), shard: 8 (over z, core).
Axes of the slice: x: 2, y: 2, z: 4, core: 2. Of those that a mesh axis runs over, the one named last changes fastest.
Arguments:
- hidden_in: bfloat16 [8, 512, 2048], P('shard', 'ctx'), may hold values from -6 to 6
- out_cot: bfloat16 [8, 512, 2048], P('shard', 'ctx'), may hold values from -6 to 6
- routes: int32 [8, 512, 8], P('shard', 'ctx'), may hold values from 0 to 31, all different within a row; in each aligned block of 128 rows (0 to 127, 128 to 255, ..., all dimensions but the last counted through in order) at most 34 rows name the same one
- block_pairs: int32 [4], replicated, may hold values from 0 to 3, each once
- norm_attn: bfloat16 [2048], P('shard'), may hold values from 0.099609375 to 1.8984375
- norm_moe: bfloat16 [2048], P('shard'), may hold values from 0.099609375 to 1.8984375
- q_gain: bfloat16 [128], P('shard'), may hold values from 0.25 to 1.75
- k_gain: bfloat16 [128], P('shard'), may hold values from 0.25 to 1.75
- w_query: bfloat16 [2048, 4096], P('shard'), may hold values from -0.125 to 0.125
- key_weight_matrix: bfloat16 [2048, 512], P('shard'), may hold values from -0.125 to 0.125
- value_weight_matrix: bfloat16 [2048, 512], P('shard'), may hold values from -0.125 to 0.125
- w_out: bfloat16 [4096, 2048], P('shard'), may hold values from -1.5 to 1.5
- w_router: bfloat16 [2048, 32], P('shard'), may hold values from -0.03125 to 0.03125
- expert_gate: bfloat16 [32, 2048, 768], P(('ctx', 'shard')), may hold values from -0.125 to 0.125
- expert_up: bfloat16 [32, 2048, 768], P(('ctx', 'shard')), may hold values from -0.125 to 0.125
- expert_down: bfloat16 [32, 768, 2048], P(('ctx', 'shard')), may hold values from -0.4375 to 0.4375
Outputs:
- block_out: bfloat16 [8, 512, 2048], P('shard', 'ctx')
- grad_in: float32 [8, 512, 2048], P('shard', 'ctx')
- grad_query: float32 [2048, 4096], P('shard')
- grad_key: float32 [2048, 512], P('shard')
- grad_value: float32 [2048, 512], P('shard')
- grad_out: float32 [4096, 2048], P('shard')
- grad_router: float32 [2048, 32], P('shard')
- grad_norm_attn: float32 [2048], P('shard')
- grad_norm_moe: float32 [2048], P('shard')
- grad_q_gain: float32 [128], P('shard')
- grad_k_gain: float32 [128], P('shard')
- grad_expert_gate: float32 [32, 2048, 768], P(('ctx', 'shard'))
- grad_expert_up: float32 [32, 2048, 768], P(('ctx', 'shard'))
- grad_expert_down: float32 [32, 768, 2048], P(('ctx', 'shard'))
The draws below stay inside these ranges and needn't reach their ends.
Inputs may be any that keep to these rules, and one draw needn't show every extreme that they name: `routes`: each row names 8 different experts; within the 128 rows of one device no expert is named by more than 34 rows, a bound that some block reaches. A permutation: ctx index c holds causal blocks p and 7 - p of its sequence, p = block_pairs[c].
All inputs are finite; a program needn't handle non-finite values.
Results may differ from the reference program's by a relative error of at most 0.023.
Values may be sent and summed in bfloat16 or wider, within the bound.
No kernel may reach another device: no remote copies, remote signals or barrier semaphores. Data moves between devices by JAX's collectives and lax.ppermute only.
A program may use at most 256 MiB of HBM per device.

```python
import math
import jax
import jax.numpy as jnp
import numpy as np
from jax import lax

MODEL_WIDTH = 2048
QUERY_HEADS = 32
KEY_VALUE_HEADS = 4
HEAD_SIZE = 128
FF = 768
TOP = 8
TOK_DEV = 128
EXPERTS = 32
SEQUENCE_TOKENS = 512
SEQUENCE_COUNT = 8
PAIRS = 4
CAP = 34
ROWS = 1088
N_SHARD = 8


def block_levels(own_key, extent, shards, smallest, high):
    loudness = 1.0
    for dim, shards_of in shards:
        heights = jax.random.uniform(jax.random.fold_in(jax.random.fold_in(own_key, 6), dim), (shards_of,), jnp.float32, smallest / len(shards), high / len(shards))
        loudness = loudness * jnp.repeat(jnp.exp(heights), extent[dim] // shards_of).reshape((-1,) + (1,) * (len(extent) - 1 - dim))
    return loudness


def routed_block(key, own, number, rows, number_of, top, limit, skew):
    ranking = jax.random.permutation(key, number_of)
    crowded, usual = load_shares(number_of, rows * top, limit, skew, True), load_shares(number_of, rows * top, limit, skew, False)
    places = jnp.arange(number_of)

    def named(tallies, offset_by):
        used = int((tallies > 0).sum())
        fixed = max(1, used // 4)
        moved = fixed + (places - fixed + offset_by * (used - fixed)) % max(1, number_of - fixed)
        return jnp.zeros((number_of,), jnp.int32).at[ranking[jnp.where(places < fixed, places, moved)]].set(jnp.asarray(tallies, jnp.int32))

    tallies = jnp.where(number % 4 == 0, named(crowded, number // 4), named(usual, number - number // 4 - 1))
    mixed = jax.random.permutation(jax.random.fold_in(own, 3), number_of)
    donor, taker = mixed[0:number_of // 2 * 2:2], mixed[1:number_of // 2 * 2:2]
    slack = jnp.minimum(tallies[donor] - 1, limit - tallies[taker]) // 2
    slack = jnp.where((donor == ranking[0]) | (taker == ranking[0]) | (tallies[taker] == 0), 0, jnp.maximum(slack, 0))
    moved = jax.random.randint(jax.random.fold_in(own, 4), (number_of // 2,), 0, 1 << 20) % (slack + 1)
    tallies = tallies.at[donor].add(-moved).at[taker].add(moved)
    labels = jnp.searchsorted(jnp.cumsum(tallies), jnp.arange(rows * top), side="right").astype(jnp.int32)
    grid = labels.reshape(top, rows).T
    grid = grid[jax.random.permutation(jax.random.fold_in(own, 1), rows)]
    offset_by = jax.random.randint(jax.random.fold_in(own, 2), (rows, 1), 0, top)
    return jnp.take_along_axis(grid, (jnp.arange(top)[None, :] + offset_by) % top, axis=1)


def load_shares(amount, total, bound, lean, full):
    loads = [(1 << 20) // math.isqrt(standing ** lean) + 1 for standing in range(1, amount + 1)]
    largest = bound if full else min(bound, max(-(-total // amount), total * loads[0] // sum(loads)))
    least = 1 if total - largest >= amount - 1 else 0
    given, surplus = [largest] + [least] * (amount - 1), total - largest - least * (amount - 1)
    while surplus > 0:
        free = [i for i in range(1, amount) if given[i] < largest] or [i for i in range(1, amount) if given[i] < bound]
        mass, budget = sum([loads[i] for i in free]), surplus
        for i in free:
            addition = min(bound - given[i], max(1, budget * loads[i] // mass), surplus)
            given[i] = given[i] + addition
            surplus = surplus - addition
    return np.array(given)


def bell_draw(key, extent, deviation, reach, shards=(), held_as=jnp.bfloat16):
    loudness = block_levels(key, extent, shards, -0.22, 0.18) if shards else 1.0
    values = jax.random.normal(key, extent, jnp.float32) * deviation * loudness
    return jnp.minimum(jnp.maximum(values, -reach), reach).astype(held_as)


def setup_inputs(seed: int = 0) -> dict:
    arg_keys = jax.random.split(jax.random.key(seed), 17)
    hidden_in = bell_draw(arg_keys[0], (SEQUENCE_COUNT, SEQUENCE_TOKENS, MODEL_WIDTH), 1.0, 6.0, ((0, 8), (1, 4)))
    out_cot = bell_draw(arg_keys[1], (SEQUENCE_COUNT, SEQUENCE_TOKENS, MODEL_WIDTH), 1.0, 6.0, ((0, 8), (1, 4)))
    routes_keys = jax.random.split(jax.random.fold_in(arg_keys[2], 1), SEQUENCE_COUNT * SEQUENCE_TOKENS // TOK_DEV)
    routes_turns = jax.random.permutation(jax.random.fold_in(arg_keys[2], 3), SEQUENCE_COUNT * SEQUENCE_TOKENS // TOK_DEV)
    routes = jax.vmap(lambda own, number: routed_block(jax.random.fold_in(arg_keys[2], 2), own, number, TOK_DEV, EXPERTS, TOP, CAP, 1))(routes_keys, routes_turns).reshape((SEQUENCE_COUNT, SEQUENCE_TOKENS, TOP))
    block_pairs = jax.random.permutation(arg_keys[3], PAIRS).astype(jnp.int32)
    norm_attn = jnp.clip(1.0 + 0.18 * jax.random.normal(arg_keys[4], (MODEL_WIDTH,), jnp.float32), 0.099609375, 1.8984375).astype(jnp.bfloat16)
    norm_moe = jnp.clip(1.0 + 0.18 * jax.random.normal(arg_keys[5], (MODEL_WIDTH,), jnp.float32), 0.099609375, 1.8984375).astype(jnp.bfloat16)
    q_gain = jnp.clip(1.0 + 0.15 * jax.random.normal(arg_keys[6], (HEAD_SIZE,), jnp.float32), 0.25, 1.75).astype(jnp.bfloat16)
    k_gain = jnp.clip(1.0 + 0.15 * jax.random.normal(arg_keys[7], (HEAD_SIZE,), jnp.float32), 0.25, 1.75).astype(jnp.bfloat16)
    w_query = bell_draw(arg_keys[8], (MODEL_WIDTH, QUERY_HEADS * HEAD_SIZE), MODEL_WIDTH ** -0.5, 0.125, ((0, 8),))
    key_weight_matrix = bell_draw(arg_keys[9], (MODEL_WIDTH, KEY_VALUE_HEADS * HEAD_SIZE), MODEL_WIDTH ** -0.5, 0.125, ((0, 8),))
    value_weight_matrix = bell_draw(arg_keys[10], (MODEL_WIDTH, KEY_VALUE_HEADS * HEAD_SIZE), MODEL_WIDTH ** -0.5, 0.125, ((0, 8),))
    w_out = bell_draw(arg_keys[11], (QUERY_HEADS * HEAD_SIZE, MODEL_WIDTH), (QUERY_HEADS * HEAD_SIZE // 256) ** -0.5, 1.5, ((0, 8),))
    w_router = bell_draw(arg_keys[12], (MODEL_WIDTH, EXPERTS), (MODEL_WIDTH * 16) ** -0.5, 0.03125, ((0, 8),))
    expert_gate = bell_draw(arg_keys[13], (EXPERTS, MODEL_WIDTH, FF), MODEL_WIDTH ** -0.5, 0.125, ((0, 32),))
    expert_up = bell_draw(arg_keys[14], (EXPERTS, MODEL_WIDTH, FF), MODEL_WIDTH ** -0.5, 0.125, ((0, 32),))
    expert_down = bell_draw(arg_keys[15], (EXPERTS, FF, MODEL_WIDTH), (FF // 4) ** -0.5, 0.4375, ((0, 32),))
    return dict(hidden_in=hidden_in, out_cot=out_cot, routes=routes, block_pairs=block_pairs, norm_attn=norm_attn, norm_moe=norm_moe, q_gain=q_gain, k_gain=k_gain, w_query=w_query, key_weight_matrix=key_weight_matrix, value_weight_matrix=value_weight_matrix, w_out=w_out, w_router=w_router, expert_gate=expert_gate, expert_up=expert_up, expert_down=expert_down)


EPS = 1e-06
THETA = 1000000.0
MASKED = -1e+30

@jax.custom_vjp
def reduced_precision(v):
    return lax.optimization_barrier(v.astype(jnp.bfloat16)).astype(jnp.float32)

@jax.custom_vjp
def low_back(v):
    return v

def low_keep(v):
    return (reduced_precision(v), None)

def low_pass(kept, grad):
    return (grad,)

def back_keep(v):
    return (v, None)

def back_low(kept, grad):
    return (reduced_precision(grad),)
reduced_precision.defvjp(low_keep, low_pass)
low_back.defvjp(back_keep, back_low)

def root_mean_square_norm(values_in, gain_vec):
    return values_in * lax.rsqrt(lax.optimization_barrier(jnp.mean(values_in * values_in, axis=-1, keepdims=True)) + EPS) * gain_vec

def rotary_embed(values_in, cosine_lookup, sine_lookup):
    half_width = values_in.shape[-1] // 2
    first_half = values_in[..., :half_width]
    second_half = values_in[..., half_width:]
    return jnp.concatenate([first_half * cosine_lookup - second_half * sine_lookup, second_half * cosine_lookup + first_half * sine_lookup], axis=-1)

def place_rows(pair_value, row_count, pair_count):
    row_ids = jnp.arange(row_count, dtype=jnp.int32)
    half_rows = row_count // 2
    block_ids = jnp.where(row_ids >= half_rows, 2 * pair_count - 1 - pair_value, pair_value)
    return (block_ids * half_rows + row_ids % half_rows).astype(jnp.int32)

def angles(positions, head_width):
    frequency = THETA ** (-(jnp.arange(head_width // 2, dtype=jnp.float32) * 2.0) / head_width)
    phase_angle = positions.astype(jnp.float32)[:, None] * frequency[None, :]
    return (jnp.cos(phase_angle)[:, None, :], jnp.sin(phase_angle)[:, None, :])

def slot_rows(route_block, expert_count):
    flat_ids = route_block.reshape(-1)
    expert_hits = (flat_ids[:, None] == jnp.arange(expert_count, dtype=jnp.int32)[None, :]).astype(jnp.int32)
    before = jnp.cumsum(expert_hits, axis=0) - expert_hits
    return (flat_ids, lax.optimization_barrier(jnp.sum(before * expert_hits, axis=1)).astype(jnp.int32))

def reference(hidden_in, out_cot, routes, block_pairs, norm_attn, norm_moe, q_gain, k_gain, w_query, key_weight_matrix, value_weight_matrix, w_out, w_router, expert_gate, expert_up, expert_down):
    highest = lax.Precision.HIGHEST
    query_groups = QUERY_HEADS // KEY_VALUE_HEADS
    score_scale = 1.0 / math.sqrt(HEAD_SIZE)
    positions = jax.vmap(lambda pair_value: place_rows(pair_value, TOK_DEV, PAIRS))(block_pairs).reshape(SEQUENCE_TOKENS)
    cosine_lookup, sine_lookup = angles(positions, HEAD_SIZE)
    cosine_slice = jnp.tile(cosine_lookup, (SEQUENCE_COUNT, 1, 1))
    sine_slice = jnp.tile(sine_lookup, (SEQUENCE_COUNT, 1, 1))
    allowed = positions[:, None] >= positions[None, :]
    flat_ids, slot_index = jax.vmap(jax.vmap(lambda route_block: slot_rows(route_block, EXPERTS)))(routes.reshape(SEQUENCE_COUNT, PAIRS, TOK_DEV, TOP))
    source = jnp.arange(PAIRS, dtype=jnp.int32)[None, :] * N_SHARD + jnp.arange(SEQUENCE_COUNT, dtype=jnp.int32)[:, None]
    target = (flat_ids * ROWS + source[:, :, None] * CAP + slot_index).reshape(-1).astype(jnp.int32)
    route_hits = routes.reshape(-1, TOP)[:, :, None] == jnp.arange(EXPERTS, dtype=jnp.int32)[None, None, :]

    def causal_attention(parts):
        query_sequence, key_seq, value_seq = parts
        grouped_queries = query_sequence.reshape(SEQUENCE_TOKENS, KEY_VALUE_HEADS, query_groups, HEAD_SIZE)
        score = low_back(jnp.einsum('qngd,knd->ngqk', grouped_queries, key_seq, precision=highest) * score_scale)
        score = jnp.where(allowed, score, MASKED)
        row_peak = lax.optimization_barrier(jnp.max(score, axis=-1, keepdims=True))
        exponent = jnp.exp(score - row_peak)
        prob_low = reduced_precision(exponent / lax.optimization_barrier(jnp.sum(exponent, axis=-1, keepdims=True)))
        return jnp.einsum('ngqk,knd->qngd', prob_low, value_seq, precision=highest)

    def layer(inputs, gain_attn, gain_moe, gain_query, key_gain_vector, mat_query, mat_key, mat_value, mat_out, mat_router, mat_gate, mat_up, mat_down):
        rows_all = inputs.reshape(-1, MODEL_WIDTH)
        normed_one = reduced_precision(root_mean_square_norm(rows_all, gain_attn))
        query_pre = low_back(jnp.dot(normed_one, mat_query, precision=highest))
        key_projected = low_back(jnp.dot(normed_one, mat_key, precision=highest))
        value_rows = reduced_precision(low_back(jnp.dot(normed_one, mat_value, precision=highest)))
        query_rows = reduced_precision(rotary_embed(root_mean_square_norm(query_pre.reshape(-1, QUERY_HEADS, HEAD_SIZE), gain_query), cosine_slice, sine_slice))
        key_rows = reduced_precision(rotary_embed(root_mean_square_norm(key_projected.reshape(-1, KEY_VALUE_HEADS, HEAD_SIZE), key_gain_vector), cosine_slice, sine_slice))
        mixed_output_rows = lax.map(jax.checkpoint(causal_attention), (query_rows.reshape(SEQUENCE_COUNT, SEQUENCE_TOKENS, QUERY_HEADS, HEAD_SIZE), key_rows.reshape(SEQUENCE_COUNT, SEQUENCE_TOKENS, KEY_VALUE_HEADS, HEAD_SIZE), value_rows.reshape(SEQUENCE_COUNT, SEQUENCE_TOKENS, KEY_VALUE_HEADS, HEAD_SIZE)))
        mixed_output_rows = reduced_precision(low_back(mixed_output_rows.reshape(-1, QUERY_HEADS * HEAD_SIZE)))
        residual = rows_all + low_back(jnp.dot(mixed_output_rows, mat_out, precision=highest))
        normed_two = reduced_precision(root_mean_square_norm(residual, gain_moe))
        logits = low_back(jnp.dot(normed_two, mat_router, precision=highest))
        chosen = lax.optimization_barrier(jnp.sum(jnp.where(route_hits, logits[:, None, :], 0.0), axis=-1))
        chosen_peak = lax.optimization_barrier(jnp.max(chosen, axis=-1, keepdims=True))
        chosen_exp = jnp.exp(chosen - chosen_peak)
        gate_weights = chosen_exp / lax.optimization_barrier(jnp.sum(chosen_exp, axis=-1, keepdims=True))
        copies = jnp.repeat(normed_two, TOP, axis=0)
        buffer = jnp.zeros((EXPERTS * ROWS, MODEL_WIDTH), normed_two.dtype).at[target].set(copies)
        buffer = low_back(buffer).reshape(EXPERTS, ROWS, MODEL_WIDTH)
        gate_pre = low_back(jnp.einsum('erd,edf->erf', buffer, mat_gate, precision=highest))
        up_pre = low_back(jnp.einsum('erd,edf->erf', buffer, mat_up, precision=highest))
        hidden_act = reduced_precision(gate_pre * jax.nn.sigmoid(gate_pre) * up_pre)
        out_rows = reduced_precision(low_back(jnp.einsum('erf,efd->erd', hidden_act, mat_down, precision=highest))).reshape(EXPERTS * ROWS, MODEL_WIDTH)
        picked = out_rows[target].reshape(-1, TOP, MODEL_WIDTH)
        mixture = lax.optimization_barrier(jnp.sum(gate_weights[:, :, None] * picked, axis=1))
        return (residual + mixture).reshape(SEQUENCE_COUNT, SEQUENCE_TOKENS, MODEL_WIDTH)
    primals = tuple((item.astype(jnp.float32) for item in (hidden_in, norm_attn, norm_moe, q_gain, k_gain, w_query, key_weight_matrix, value_weight_matrix, w_out, w_router, expert_gate, expert_up, expert_down)))
    result, pullback = jax.vjp(layer, *primals)
    grads = pullback(out_cot.astype(jnp.float32))
    return (result.astype(jnp.bfloat16), grads[0], grads[5], grads[6], grads[7], grads[8], grads[9], grads[1], grads[2], grads[3], grads[4], grads[10], grads[11], grads[12])
```

```python
import math

import jax
import jax.numpy as jnp
from jax import lax
from jax.experimental import pallas as pl
from jax.experimental.pallas import tpu as pltpu
from jax.sharding import PartitionSpec as P


QUERY_HEADS = 32
KEY_VALUE_HEADS = 4
HEAD_SIZE = 128
TOP = 8

EPS = 1e-06
THETA = 1000000.0
MASKED = -1e30
LANES = 128
VMEM_LIMIT = 58 * 1024 * 1024
F32 = jnp.float32
BF16 = jnp.bfloat16


def dot(a, b, ca=1, cb=0):
    return lax.dot_general(a, b, (((ca,), (cb,)), ((), ())), preferred_element_type=F32)


def params(**kw):
    return pltpu.CompilerParams(vmem_limit_bytes=VMEM_LIMIT, **kw)


def inverse_rms(v):
    return lax.rsqrt(jnp.mean(v * v, axis=-1, keepdims=True) + EPS)


def turn(v, cosine, sine):
    return v * cosine + pltpu.roll(v, HEAD_SIZE // 2, 1) * sine


def head(pre, gain, cosine, sine):
    return turn(pre * inverse_rms(pre) * gain, cosine, sine).astype(BF16)


def head_back(grad, pre, gain, cosine, sine):
    g = turn(grad, cosine, -sine)
    r = inverse_rms(pre)
    n = pre * r
    scaled = g * gain
    back = r * (scaled - n * jnp.mean(n * scaled, axis=-1, keepdims=True))
    return back.astype(BF16), jnp.sum(g * n, axis=0, keepdims=True)


def attend_forward(qkv, heads, gains, cosine, sine, pos_col, pos_row):
    n = qkv.shape[0]
    hs = HEAD_SIZE
    factor = math.log2(math.e) / math.sqrt(HEAD_SIZE)

    def kernel(q_ref, k_ref, v_ref, gain_ref, cos_ref, sin_ref, pc_ref, pr_ref, out_ref, tot_ref, key_s, val_s, bias_s):
        h = pl.program_id(0)

        @pl.when(h == 0)
        def _():
            key_s[...] = head(k_ref[...], gain_ref[1:2, :], cos_ref[...], sin_ref[...])
            val_s[:, :hs] = v_ref[...].astype(BF16)
            val_s[:, hs:] = jnp.ones((n, hs), BF16)
            bias_s[...] = jnp.where(pc_ref[...] >= pr_ref[...], 0.0, MASKED)
            tot_ref[...] = jnp.zeros_like(tot_ref)

        q = head(q_ref[...], gain_ref[0:1, :], cos_ref[...], sin_ref[...])
        e = jnp.exp2(dot(q, key_s[...], 1, 1) * factor + bias_s[...]).astype(BF16)
        both = dot(e, val_s[...])
        inverse = 1.0 / both[:, hs:]
        out_ref[...] = (both[:, :hs] * inverse).astype(BF16)
        lane = lax.broadcasted_iota(jnp.int32, (n, hs), 1)
        tot_ref[...] = jnp.where(lane == h, inverse, tot_ref[...])

    full = lambda a: pl.BlockSpec(a.shape, lambda h: (0, 0))
    return pl.pallas_call(
        kernel,
        grid=(heads,),
        in_specs=[
            pl.BlockSpec((n, hs), lambda h: (0, h)),
            pl.BlockSpec((n, hs), lambda h: (0, heads)),
            pl.BlockSpec((n, hs), lambda h: (0, heads + 1)),
            full(gains),
            full(cosine),
            full(sine),
            full(pos_col),
            full(pos_row),
        ],
        out_specs=[pl.BlockSpec((n, hs), lambda h: (0, h)), pl.BlockSpec((n, hs), lambda h: (0, 0))],
        out_shape=[
            jax.ShapeDtypeStruct((n, heads * hs), BF16),
            jax.ShapeDtypeStruct((n, hs), F32),
        ],
        scratch_shapes=[pltpu.VMEM((n, hs), BF16), pltpu.VMEM((n, 2 * hs), BF16), pltpu.VMEM((n, n), F32)],
        compiler_params=params(),
        name="attend_forward",
    )(qkv, qkv, qkv, gains, cosine, sine, pos_col, pos_row)


def attend_backward(qkv, d_mix, mix, totals, heads, gains, cosine, sine, pos_col, pos_row):
    n = qkv.shape[0]
    hs = HEAD_SIZE
    scale = 1.0 / math.sqrt(HEAD_SIZE)
    factor = math.log2(math.e) / math.sqrt(HEAD_SIZE)

    def kernel(q_ref, k_ref, v_ref, dm_ref, mix_ref, tot_ref, gain_ref, cos_ref, sin_ref, pc_ref, pr_ref, dq_ref, dkv_ref, gg_ref, key_s, val_s, dk_s, dv_s, bias_s):
        h = pl.program_id(0)

        @pl.when(h == 0)
        def _():
            key_s[...] = head(k_ref[...], gain_ref[1:2, :], cos_ref[...], sin_ref[...])
            val_s[...] = v_ref[...].astype(BF16)
            bias_s[...] = jnp.where(pc_ref[...] >= pr_ref[...], 0.0, MASKED)
            dk_s[...] = jnp.zeros_like(dk_s)
            dv_s[...] = jnp.zeros_like(dv_s)
            gg_ref[...] = jnp.zeros_like(gg_ref)

        pre = q_ref[...]
        q = head(pre, gain_ref[0:1, :], cos_ref[...], sin_ref[...])
        dm = dm_ref[...]
        lane = lax.broadcasted_iota(jnp.int32, (n, hs), 1)
        inverse = jnp.sum(jnp.where(lane == h, tot_ref[...], 0.0), axis=-1, keepdims=True)
        centre = jnp.sum(dm.astype(F32) * mix_ref[...].astype(F32), axis=-1, keepdims=True)
        p = jnp.exp2(dot(q, key_s[...], 1, 1) * factor + bias_s[...]) * inverse
        dp = dot(dm, val_s[...], 1, 1)
        ds = (p * (dp - centre)).astype(BF16)
        dq = dot(ds, key_s[...]) * scale
        dk_s[...] += dot(ds, q, 0, 0)
        dv_s[...] += dot(p.astype(BF16), dm, 0, 0)
        back, gg = head_back(dq, pre, gain_ref[0:1, :], cos_ref[...], sin_ref[...])
        dq_ref[...] = back
        gg_ref[0:1, :] += gg

        @pl.when(h == heads - 1)
        def _():
            back, gg = head_back(
                dk_s[...] * scale, k_ref[...], gain_ref[1:2, :], cos_ref[...], sin_ref[...]
            )
            dkv_ref[:, :hs] = back
            dkv_ref[:, hs:] = dv_s[...].astype(BF16)
            gg_ref[1:2, :] = gg

    full = lambda a: pl.BlockSpec(a.shape, lambda h: (0, 0))
    col = pl.BlockSpec((n, hs), lambda h: (0, h))
    return pl.pallas_call(
        kernel,
        grid=(heads,),
        in_specs=[
            col,
            pl.BlockSpec((n, hs), lambda h: (0, heads)),
            pl.BlockSpec((n, hs), lambda h: (0, heads + 1)),
            col,
            col,
            full(totals),
            full(gains),
            full(cosine),
            full(sine),
            full(pos_col),
            full(pos_row),
        ],
        out_specs=[col, pl.BlockSpec((n, 2 * hs), lambda h: (0, 0)), pl.BlockSpec((8, hs), lambda h: (0, 0))],
        out_shape=[
            jax.ShapeDtypeStruct((n, heads * hs), BF16),
            jax.ShapeDtypeStruct((n, 2 * hs), BF16),
            jax.ShapeDtypeStruct((8, hs), F32),
        ],
        scratch_shapes=[
            pltpu.VMEM((n, hs), BF16),
            pltpu.VMEM((n, hs), BF16),
            pltpu.VMEM((n, hs), F32),
            pltpu.VMEM((n, hs), F32),
            pltpu.VMEM((n, n), F32),
        ],
        compiler_params=params(),
        name="attend_backward",
    )(qkv, qkv, qkv, d_mix, mix, totals, gains, cosine, sine, pos_col, pos_row)


def expert_piece(x, cot, router, wg, wu, wd, me, experts, back_extra):
    r, d = x.shape
    f = wg.shape[1]
    extra = cot.shape[1] - d

    def kernel(me_ref, x_ref, cot_ref, router_ref, wg_ref, wu_ref, wd_ref,
               mixed_ref, back_ref, hid_ref, deo_ref, dg_ref, du_ref):
        own = me_ref[0]
        xv = x_ref[...]
        lane = lax.broadcasted_iota(jnp.int32, (r, extra), 1)
        mask = (cot_ref[:, d:].astype(F32) > 0.5) & (lane < experts)
        kept = jnp.where(mask, dot(xv, router_ref[...]), MASKED)
        e = jnp.where(mask, jnp.exp(kept - jnp.max(kept, axis=-1, keepdims=True)), 0.0)
        total = jnp.sum(e, axis=-1, keepdims=True)
        gate = jnp.sum(jnp.where(lane == own, e, 0.0), axis=-1, keepdims=True) / jnp.where(total > 0.0, total, 1.0)
        gp = dot(xv, wg_ref[...])
        up = dot(xv, wu_ref[...])
        sig = jax.nn.sigmoid(gp)
        silu = gp * sig
        hid = (silu * up).astype(BF16)
        hid_ref[...] = hid
        eo = dot(hid, wd_ref[...]).astype(BF16).astype(F32)
        dout = cot_ref[:, :d].astype(F32)
        dgr = jnp.sum(dout * eo, axis=-1, keepdims=True)
        mixed_ref[...] = (gate * eo).astype(BF16)
        deo = (gate * dout).astype(BF16)
        deo_ref[...] = deo
        dh = dot(deo, wd_ref[...], 1, 1)
        dg = (dh * up * sig * (1.0 + gp * (1.0 - sig))).astype(BF16)
        du = (dh * silu).astype(BF16)
        dg_ref[...] = dg
        du_ref[...] = du
        back_ref[:, :d] = (dot(dg, wg_ref[...], 1, 1) + dot(du, wu_ref[...], 1, 1)).astype(BF16)
        lane = lax.broadcasted_iota(jnp.int32, (r, back_extra), 1)
        high = dgr.astype(BF16).astype(F32)
        low = dgr - high
        back_ref[:, d:] = jnp.where(lane == own, high, jnp.where(lane == own + experts, low, 0.0)).astype(BF16)

    vm = pl.BlockSpec(memory_space=pltpu.VMEM)
    return pl.pallas_call(
        kernel,
        in_specs=[pl.BlockSpec(memory_space=pltpu.SMEM)] + [vm] * 6,
        out_specs=[vm] * 6,
        out_shape=[
            jax.ShapeDtypeStruct((r, d), BF16),
            jax.ShapeDtypeStruct((r, d + back_extra), BF16),
            jax.ShapeDtypeStruct((r, f), BF16),
            jax.ShapeDtypeStruct((r, d), BF16),
            jax.ShapeDtypeStruct((r, f), BF16),
            jax.ShapeDtypeStruct((r, f), BF16),
        ],
        compiler_params=params(),
        name="expert_piece",
    )(me, x, cot, router, wg, wu, wd)


def expert_grads(xs, dgs, dus, hids, deos, block=256):
    n = len(xs)
    r, d = xs[0].shape
    f = dgs[0].shape[1]

    def kernel(*refs):
        x, dg, du, hid, deo = (refs[i * n : (i + 1) * n] for i in range(5))
        gg_ref, gu_ref, gd_ref, x_s, deo_s, dg_s, du_s, hid_s = refs[5 * n :]

        @pl.when(pl.program_id(0) == 0)
        def _():
            for i in range(n):
                dg_s[i * r : (i + 1) * r, :] = dg[i][...]
                du_s[i * r : (i + 1) * r, :] = du[i][...]
                x_s[i * r : (i + 1) * r, :] = hid[i][:, :block]
            for j in range(f // block):
                if j:
                    for i in range(n):
                        x_s[i * r : (i + 1) * r, :] = hid[i][:, j * block : (j + 1) * block]
                hid_s[j * block : (j + 1) * block, :] = x_s[...].T

        for i in range(n):
            x_s[i * r : (i + 1) * r, :] = x[i][...]
            deo_s[i * r : (i + 1) * r, :] = deo[i][...]
        xt = x_s[...].T
        gg_ref[...] = dot(xt, dg_s[...])
        gu_ref[...] = dot(xt, du_s[...])
        gd_ref[...] = dot(hid_s[...], deo_s[...])

    part = pl.BlockSpec((r, block), lambda j: (0, j))
    whole = pl.BlockSpec((r, f), lambda j: (0, 0))
    return pl.pallas_call(
        kernel,
        grid=(d // block,),
        in_specs=[part] * n + [whole] * (3 * n) + [part] * n,
        out_specs=[pl.BlockSpec((block, f), lambda j: (j, 0))] * 2
        + [pl.BlockSpec((f, block), lambda j: (0, j))],
        out_shape=[jax.ShapeDtypeStruct((d, f), F32)] * 2
        + [jax.ShapeDtypeStruct((f, d), F32)],
        scratch_shapes=[
            pltpu.VMEM((n * r, block), BF16),
            pltpu.VMEM((n * r, block), BF16),
            pltpu.VMEM((n * r, f), BF16),
            pltpu.VMEM((n * r, f), BF16),
            pltpu.VMEM((f, n * r), BF16),
        ],
        compiler_params=params(),
        name="expert_grads",
    )(*xs, *dgs, *dus, *hids, *deos)


def combine(place, parts):
    n = len(parts)
    m = place.shape[0]
    r, d = parts[0].shape
    block = 256

    def kernel(place_ref, *refs):
        v, out_ref, v_s = refs[:n], refs[n], refs[n + 1]
        for i in range(n):
            v_s[i * r : (i + 1) * r, :] = v[i][...]
        out_ref[...] = dot(place_ref[...], v_s[...]).astype(BF16)

    return pl.pallas_call(
        kernel,
        grid=(pl.cdiv(d, block),),
        in_specs=[pl.BlockSpec(place.shape, lambda j: (0, 0))]
        + [pl.BlockSpec((r, block), lambda j: (0, j))] * n,
        out_specs=pl.BlockSpec((m, block), lambda j: (0, j)),
        out_shape=jax.ShapeDtypeStruct((m, d), BF16),
        scratch_shapes=[pltpu.VMEM((n * r, block), BF16)],
        compiler_params=params(),
    )(place, *parts)


def assemble(parts, c, qc, share):
    n = len(parts)
    rows = parts[0].shape[0]
    hs = HEAD_SIZE
    kw = n // share * hs

    def kernel(c_ref, *refs):
        v = refs[:n]
        q_ref, k_ref, v_ref, small_ref = refs[n:]
        small_ref[...] = sum(v[d][:, qc + 2 * hs :].astype(F32) for d in range(n))
        if share > 1:
            k_ref[...] = jnp.zeros_like(k_ref)
            v_ref[...] = jnp.zeros_like(v_ref)
        for d in range(n):
            at = c_ref[0] ^ d
            q_ref[:, pl.ds(pl.multiple_of(at * qc, qc), qc)] = v[d][:, :qc].astype(F32)
            to = pl.ds(pl.multiple_of(at // share * hs, hs), hs)
            key = v[d][:, qc : qc + hs].astype(F32)
            val = v[d][:, qc + hs : qc + 2 * hs].astype(F32)
            if share > 1:
                k_ref[:, to] += key
                v_ref[:, to] += val
            else:
                k_ref[:, to] = key
                v_ref[:, to] = val

    vm = pl.BlockSpec(memory_space=pltpu.VMEM)
    return pl.pallas_call(
        kernel,
        in_specs=[pl.BlockSpec(memory_space=pltpu.SMEM)] + [vm] * n,
        out_specs=[vm] * 4,
        out_shape=[
            jax.ShapeDtypeStruct((rows, n * qc), F32),
            jax.ShapeDtypeStruct((rows, kw), F32),
            jax.ShapeDtypeStruct((rows, kw), F32),
            jax.ShapeDtypeStruct((rows, parts[0].shape[1] - qc - 2 * hs), F32),
        ],
        compiler_params=params(),
        name="assemble",
    )(c, *parts)


def weight_grads(h1, d_q, d_kv, small, block=256):
    n, d = h1.shape
    qc, kc, sc = d_q.shape[1], d_kv.shape[1], small.shape[1]

    def kernel(h_ref, q_ref, kv_ref, small_ref, out_ref):
        h = h_ref[...].T
        out_ref[:, :qc] = dot(h, q_ref[...], 1, 0).astype(BF16)
        out_ref[:, qc : qc + kc] = dot(h, kv_ref[...], 1, 0).astype(BF16)
        out_ref[:, qc + kc :] = small_ref[...]

    return pl.pallas_call(
        kernel,
        grid=(d // block,),
        in_specs=[
            pl.BlockSpec((n, block), lambda j: (0, j)),
            pl.BlockSpec((n, qc), lambda j: (0, 0)),
            pl.BlockSpec((n, kc), lambda j: (0, 0)),
            pl.BlockSpec((block, sc), lambda j: (j, 0)),
        ],
        out_specs=pl.BlockSpec((block, qc + kc + sc), lambda j: (j, 0)),
        out_shape=jax.ShapeDtypeStruct((d, qc + kc + sc), BF16),
        compiler_params=params(),
        name="weight_grads",
    )(h1, d_q, d_kv, small)


def assemble_columns(parts, c):
    n = len(parts)
    rows, w = parts[0].shape

    def kernel(c_ref, *refs):
        for d in range(n):
            at = pl.multiple_of((c_ref[0] ^ d) * w, w)
            refs[n][:, pl.ds(at, w)] = refs[d][...].astype(F32)

    vm = pl.BlockSpec(memory_space=pltpu.VMEM)
    return pl.pallas_call(
        kernel,
        in_specs=[pl.BlockSpec(memory_space=pltpu.SMEM)] + [vm] * n,
        out_specs=vm,
        out_shape=jax.ShapeDtypeStruct((rows, n * w), F32),
        compiler_params=params(),
        name="assemble_columns",
    )(c, *parts)


def plan(targets, rows, block=LANES):
    n, m = targets.shape

    def kernel(row_ref, col_ref, *outs):
        ids = lax.broadcasted_iota(jnp.int32, (rows, block), 0)
        for d in range(n):
            outs[d][...] = jnp.where(row_ref[d : d + 1, :] == ids, 1.0, 0.0).astype(BF16)
        ids = lax.broadcasted_iota(jnp.int32, (block, n * rows), 1)
        hot = col_ref[:, 0:1] == ids
        for d in range(1, n):
            hot = hot | (col_ref[:, d : d + 1] + d * rows == ids)
        outs[n][...] = jnp.where(hot, 1.0, 0.0).astype(BF16)

    return pl.pallas_call(
        kernel,
        grid=(m // block,),
        in_specs=[
            pl.BlockSpec((n, block), lambda j: (0, j)),
            pl.BlockSpec((block, n), lambda j: (j, 0)),
        ],
        out_specs=[pl.BlockSpec((rows, block), lambda j: (0, j))] * n
        + [pl.BlockSpec((block, n * rows), lambda j: (j, 0))],
        out_shape=[jax.ShapeDtypeStruct((rows, m), BF16)] * n
        + [jax.ShapeDtypeStruct((m, n * rows), BF16)],
        compiler_params=params(),
        name="plan",
    )(targets, targets.T)


def norm_rows(parts, gain):
    n = len(parts)
    t, d = parts[0].shape

    def kernel(gain_ref, *refs):
        for i in range(n):
            v = refs[i][...].astype(F32)
            refs[n][i * t : (i + 1) * t, :] = (v * inverse_rms(v) * gain_ref[...]).astype(BF16)

    vm = pl.BlockSpec(memory_space=pltpu.VMEM)
    return pl.pallas_call(
        kernel,
        in_specs=[vm] * (n + 1),
        out_specs=vm,
        out_shape=jax.ShapeDtypeStruct((n * t, d), BF16),
        compiler_params=params(),
        name="norm_rows",
    )(gain, *parts)


def out_proj(parts, w_cols, c):
    n = len(parts)
    t, k = parts[0].shape
    w = w_cols.shape[1]

    def kernel(c_ref, *refs):
        w_ref, out_ref, acc_ref = refs[n:]
        d = pl.program_id(0)
        for i in range(n):

            @pl.when(d == i)
            def _():
                part = dot(refs[i][...], w_ref[...])
                for b in range(n):
                    to, of = b * (t // n), (b ^ i) * (t // n)
                    block = part[of : of + t // n, :]
                    if i == 0:
                        acc_ref[to : to + t // n, :] = block
                    elif i < n - 1:
                        acc_ref[to : to + t // n, :] += block
                    else:
                        total = acc_ref[to : to + t // n, :] + block
                        out_ref[to : to + t // n, :] = total.astype(BF16)

    return pl.pallas_call(
        kernel,
        grid_spec=pltpu.PrefetchScalarGridSpec(
            num_scalar_prefetch=1,
            grid=(n,),
            in_specs=[pl.BlockSpec((t, k), lambda d, c_ref: (0, 0))] * n
            + [pl.BlockSpec((k, w), lambda d, c_ref: (c_ref[0] ^ d, 0))],
            out_specs=pl.BlockSpec((t, w), lambda d, c_ref: (0, 0)),
            scratch_shapes=[pltpu.VMEM((t, w), F32)],
        ),
        out_shape=jax.ShapeDtypeStruct((t, w), BF16),
        compiler_params=params(),
        name="out_proj",
    )(c, *parts, w_cols)


def out_grads(mixes, d_parts, c, block=256):
    n = len(mixes)
    t, k = mixes[0].shape
    rows, d_model = d_parts[0].shape
    w = d_model // n
    nb = k // block

    def kernel(c_ref, *refs):
        mix, dp, out_ref, d_s = refs[:n], refs[n : 2 * n], refs[2 * n], refs[2 * n + 1]
        i, j = pl.program_id(0), pl.program_id(1)

        @pl.when((i == 0) & (j == 0))
        def _():
            for e in range(n):
                for b in range(n):
                    d_s[e, b * rows : (b + 1) * rows, :] = dp[b ^ e][...]

        for e in range(n):

            @pl.when(i == e)
            def _():
                m = mix[e][:, pl.ds(pl.multiple_of(j * block, block), block)]
                out_ref[...] = dot(m.T, d_s[e]).astype(BF16)

    return pl.pallas_call(
        kernel,
        grid_spec=pltpu.PrefetchScalarGridSpec(
            num_scalar_prefetch=1,
            grid=(n, nb),
            in_specs=[pl.BlockSpec((t, k), lambda i, j, c_ref: (0, 0))] * n
            + [pl.BlockSpec((rows, w), lambda i, j, c_ref: (0, c_ref[0]))] * n,
            out_specs=pl.BlockSpec((block, w), lambda i, j, c_ref: ((c_ref[0] ^ i) * nb + j, 0)),
            scratch_shapes=[pltpu.VMEM((n, t, w), BF16)],
        ),
        out_shape=jax.ShapeDtypeStruct((n * k, w), BF16),
        compiler_params=params(),
        name="out_grads",
    )(c, *mixes, *d_parts)


def residual(x, parts, gain, c):
    n = len(parts)
    w = parts[0].shape[1]

    def kernel(c_ref, x_ref, gain_ref, *refs):
        r1_ref, h2_ref = refs[n:]
        for i in range(n):
            at = pl.ds(pl.multiple_of((c_ref[0] ^ i) * w, w), w)
            r1_ref[:, at] = x_ref[:, at].astype(F32) + refs[i][...].astype(F32)
        v = r1_ref[...]
        h2_ref[...] = (v * inverse_rms(v) * gain_ref[...]).astype(BF16)

    vm = pl.BlockSpec(memory_space=pltpu.VMEM)
    return pl.pallas_call(
        kernel,
        in_specs=[pl.BlockSpec(memory_space=pltpu.SMEM)] + [vm] * (n + 2),
        out_specs=[vm] * 2,
        out_shape=[jax.ShapeDtypeStruct(x.shape, F32), jax.ShapeDtypeStruct(x.shape, BF16)],
        compiler_params=params(),
        name="residual",
    )(c, x, gain, *parts)


def masked_softmax(logits, mask):
    kept = jnp.where(mask, logits, MASKED)
    e = jnp.where(mask, jnp.exp(kept - jnp.max(kept, axis=-1, keepdims=True)), 0.0)
    total = jnp.sum(e, axis=-1, keepdims=True)
    return e / jnp.where(total > 0.0, total, 1.0)


def norm_back(v, gain, grad):
    r = inverse_rms(v)
    n = v * r
    scaled = grad * gain
    back = r * (scaled - n * jnp.mean(n * scaled, axis=-1, keepdims=True))
    return back, grad * n


def turn_back(back_sum, r1, h2, cot, hits, router, gain, experts):
    t, d = r1.shape
    extra = hits.shape[1]

    def kernel(back_ref, r1_ref, h2_ref, cot_ref, hit_ref, router_ref, gain_ref, dr_ref, da_ref, gr_ref, gn_ref):
        gates = masked_softmax(
            dot(h2_ref[...], router_ref[...]), hit_ref[...].astype(F32) > 0.5
        )
        high = back_ref[:, d : d + extra].astype(F32)
        if experts % LANES:
            d_gates = high + pltpu.roll(high, extra - experts, 1)
        else:
            d_gates = high + back_ref[:, d + experts : d + experts + extra].astype(F32)
        centre = jnp.sum(gates * d_gates, axis=-1, keepdims=True)
        d_logits = (gates * (d_gates - centre)).astype(BF16)
        gr_ref[...] = dot(h2_ref[...], d_logits, 0, 0)
        d_h2 = back_ref[:, :d].astype(F32) + dot(d_logits, router_ref[...], 1, 1)
        back, gain_rows = norm_back(r1_ref[...], gain_ref[...], d_h2)
        gn_ref[...] = jnp.sum(gain_rows, axis=0, keepdims=True)
        total = cot_ref[...].astype(F32) + back
        dr_ref[...] = total
        da_ref[...] = total.astype(BF16)

    vm = pl.BlockSpec(memory_space=pltpu.VMEM)
    return pl.pallas_call(
        kernel,
        in_specs=[vm] * 7,
        out_specs=[vm] * 4,
        out_shape=[
            jax.ShapeDtypeStruct((t, d), F32),
            jax.ShapeDtypeStruct((t, d), BF16),
            jax.ShapeDtypeStruct((d, extra), F32),
            jax.ShapeDtypeStruct((1, d), F32),
        ],
        compiler_params=params(),
        name="turn_back",
    )(back_sum, r1, h2, cot, hits, router, gain)


def input_back(x, parts, d_r1, gain):
    n = len(parts)

    def kernel(x_ref, dr_ref, gain_ref, *refs):
        grad = refs[0][...].astype(F32)
        for i in range(1, n):
            grad = grad + refs[i][...].astype(F32)
        back, _ = norm_back(x_ref[...].astype(F32), gain_ref[...], grad)
        refs[n][...] = dr_ref[...] + back

    vm = pl.BlockSpec(memory_space=pltpu.VMEM)
    return pl.pallas_call(
        kernel,
        in_specs=[vm] * (n + 3),
        out_specs=vm,
        out_shape=jax.ShapeDtypeStruct(x.shape, F32),
        compiler_params=params(),
        name="input_back",
    )(x, d_r1, gain, *parts)


def round_up(n, m):
    return (n + m - 1) // m * m


def rows_of_pair(pair_value, row_count, pair_count):
    row_ids = jnp.arange(row_count, dtype=jnp.int32)
    half = row_count // 2
    block = jnp.where(row_ids >= half, 2 * pair_count - 1 - pair_value, pair_value)
    return block * half + row_ids % half


def layer(
    hidden_in,
    out_cot,
    routes,
    block_pairs,
    norm_attn,
    norm_moe,
    q_gain,
    k_gain,
    w_query,
    w_key,
    w_value,
    w_out,
    w_router,
    expert_gate,
    expert_up,
    expert_down,
):
    C = lax.axis_size("ctx")
    S = lax.axis_size("shard")
    T = hidden_in.shape[1]
    D = hidden_in.shape[2]
    E = C * S
    M = S * T
    QW = QUERY_HEADS * HEAD_SIZE
    qc = QW // C
    share = C // KEY_VALUE_HEADS
    hc = qc // HEAD_SIZE
    cap = max(2, (17 * T * TOP + 16 * E - 1) // (16 * E))
    rows = S * cap
    ws = w_query.shape[0]
    gs = q_gain.shape[0]
    po = QW // E
    c = lax.axis_index("ctx")
    s = lax.axis_index("shard")
    me = c * S + s
    c_vec = c.astype(jnp.int32).reshape(1)

    def exchange_ctx(parts):
        out = [parts[0]]
        for d in range(1, C):
            out.append(lax.ppermute(parts[d], "ctx", [(i, i ^ d) for i in range(C)]))
        return out

    def gather_ctx(v):
        return exchange_ctx([v] * C)

    def gather_shard(v):
        return lax.all_gather(v, "shard", axis=0, tiled=True)

    def sum_shard(v):
        return lax.psum_scatter(v, "shard", scatter_dimension=0, tiled=True)

    kv = c // share
    packed = jnp.concatenate(
        [
            lax.dynamic_slice_in_dim(w_query, c * qc, qc, 1),
            lax.dynamic_slice_in_dim(w_key, kv * HEAD_SIZE, HEAD_SIZE, 1),
            lax.dynamic_slice_in_dim(w_value, kv * HEAD_SIZE, HEAD_SIZE, 1),
        ],
        axis=1,
    )
    w_qkv = gather_shard(packed)
    hits = (
        (routes[0][:, :, None] == jnp.arange(E, dtype=jnp.int32)[None, None, :])
        .any(axis=1)
        .astype(BF16)
    )
    rw = ws * E // T
    nw = ws // T
    small_parts = [
        hits,
        w_router.reshape(T, rw),
        norm_moe.reshape(T, nw),
        norm_attn.reshape(T, nw),
        jnp.pad(jnp.concatenate([q_gain, k_gain]), (0, T - 2 * gs)).reshape(T, 1),
    ]
    small_width = round_up(E + rw + 2 * nw + 1, LANES)
    small_parts.append(jnp.zeros((T, small_width - E - rw - 2 * nw - 1), BF16))
    table = gather_shard(jnp.concatenate(small_parts, axis=1))
    x_own = hidden_in[0]
    x_parts = gather_ctx(x_own)
    hits_column = table[:, :E]
    router = table[:, E : E + rw].reshape(D, E)
    gain_moe = table[:, E + rw : E + rw + nw].reshape(D).astype(F32)
    gain_attn = table[:, E + rw + nw : E + rw + 2 * nw].reshape(D).astype(F32)
    head_gains = table[:, E + rw + 2 * nw].reshape(S, T).astype(F32)
    head_gains = jnp.concatenate(
        [
            head_gains[:, :gs].reshape(1, -1),
            head_gains[:, gs : 2 * gs].reshape(1, -1),
            jnp.zeros((6, HEAD_SIZE), F32),
        ],
        axis=0,
    )

    spread = [((p % C) * S + p // C, p) for p in range(E)]
    piece = lax.ppermute(lax.dynamic_slice_in_dim(w_out, c * po, po, 0), ("ctx", "shard"), spread)
    w_out_rows = gather_shard(piece)
    dc = D // C
    w_out_cols = gather_shard(lax.dynamic_slice_in_dim(w_out, c * dc, dc, 1))

    extra = round_up(E, LANES)
    hits_wide = jnp.pad(hits, ((0, 0), (0, extra - E)))
    cot_own = jnp.concatenate([out_cot[0], hits_wide], axis=1)
    cot_column = gather_shard(cot_own)
    router_wide = jnp.pad(router, ((0, 0), (0, extra - E)))

    pairs_here = jnp.stack([block_pairs[c ^ d] for d in range(C)])
    positions = jax.vmap(lambda p: rows_of_pair(p, T, C))(pairs_here).reshape(-1)
    frequency = THETA ** (-(jnp.arange(HEAD_SIZE // 2, dtype=F32) * 2.0) / HEAD_SIZE)
    phase = positions.astype(F32)[:, None] * frequency[None, :]
    cosine, sine = jnp.cos(phase), jnp.sin(phase)
    cosine = jnp.concatenate([cosine, cosine], axis=1)
    sine = jnp.concatenate([-sine, sine], axis=1)
    pos_col, pos_row = positions[:, None], positions[None, :]

    own_experts = (
        jnp.arange(E, dtype=jnp.int32)[None, :]
        == ((c ^ jnp.arange(C, dtype=jnp.int32)) * S + s)[:, None]
    ).astype(BF16)
    hit = dot(own_experts, hits_column, 1, 1).reshape(C, S, T)
    slot = (jnp.cumsum(hit, axis=2) - hit).astype(jnp.int32)
    target = jnp.where(
        hit > 0.5, jnp.arange(S, dtype=jnp.int32)[None, :, None] * cap + slot, -E * cap
    )
    *picks, place = plan(target.reshape(C, M), rows)

    h1 = norm_rows(x_parts, gain_attn.reshape(1, D))
    qkv = dot(h1, w_qkv, 1, 0)
    mix, totals = attend_forward(qkv, hc, head_gains, cosine, sine, pos_col, pos_row)
    mixes = gather_ctx(mix)
    attn_cols = out_proj(mixes, w_out_cols, c_vec).reshape(C, T, dc)
    attn_out = exchange_ctx([attn_cols[d] for d in range(C)])
    r1, h2 = residual(x_own, attn_out, gain_moe.reshape(1, D), c_vec)

    h2_column = gather_shard(h2)

    def dispatch(v):
        sent = [None] * C
        for d in [C - 1] + list(range(1, C - 1)) + [0]:
            sent[d] = dot(picks[d], v, 1, 0).astype(BF16)
        return exchange_ctx(sent)

    cot_in = dispatch(cot_column)
    expert_in = dispatch(h2_column)

    wg, wu, wd = expert_gate[0], expert_up[0], expert_down[0]
    me_vec = me.astype(jnp.int32).reshape(1)
    back_extra = round_up(2 * E, LANES)
    done = [None] * C
    for d in [0, C - 1] + list(range(1, C - 1)):
        done[d] = expert_piece(
            expert_in[d], cot_in[d], router_wide, wg, wu, wd, me_vec, E, back_extra
        )
    mixed_rows, back_rows, hidden, d_expert_out, d_gate, d_up = (list(v) for v in zip(*done))
    back_in = exchange_ctx(back_rows)
    back_sum = sum_shard(combine(place, back_in))
    mixed_in = exchange_ctx(mixed_rows)
    grad_gate, grad_up, grad_down = expert_grads(expert_in, d_gate, d_up, hidden, d_expert_out)

    d_r1, d_attn_own, grad_router, grad_norm_moe = turn_back(
        back_sum, r1, h2, out_cot[0], hits_wide, router_wide, gain_moe.reshape(1, D), E
    )
    d_attn_parts = gather_ctx(d_attn_own)
    grad_out_piece = sum_shard(out_grads(mixes, d_attn_parts, c_vec))
    d_attn = jnp.concatenate(d_attn_parts, axis=0)
    d_mix = dot(d_attn, w_out_rows, 1, 1).astype(BF16)
    d_q, d_kv, gain_grads = attend_backward(
        qkv, d_mix, mix, totals, hc, head_gains, cosine, sine, pos_col, pos_row
    )
    d_qkv = jnp.concatenate([d_q, d_kv], axis=1)

    x_seq = jnp.concatenate(x_parts, axis=0).astype(F32)
    d_h1_partial = dot(d_qkv, w_qkv, 1, 1)
    grad_norm_attn = jnp.sum(d_h1_partial * (x_seq * inverse_rms(x_seq)), axis=0)

    def shard_column(v):
        return jnp.pad(v.reshape(S, gs), ((0, 0), (0, ws - gs))).reshape(-1)

    wide = round_up(E + 4, LANES)
    lane = jnp.arange(wide, dtype=jnp.int32)[None, :]
    small = jnp.pad(grad_router[:, :E], ((0, 0), (0, wide - E)))
    columns = (
        grad_norm_attn,
        grad_norm_moe.reshape(D),
        shard_column(gain_grads[0]),
        shard_column(gain_grads[1]),
    )
    for i, v in enumerate(columns):
        small = small + jnp.where(lane == E + i, v[:, None], 0.0)
    owned_partial = weight_grads(h1, d_q, d_kv, small.astype(BF16))
    owned = sum_shard(owned_partial)

    d_h1_parts = d_h1_partial.astype(BF16).reshape(C, T, D)
    d_h1_in = exchange_ctx([d_h1_parts[d] for d in range(C)])
    grad_in = input_back(x_own, d_h1_in, d_r1, gain_attn.reshape(1, D))[None]

    mixture = sum_shard(combine(place, mixed_in)).astype(F32)
    block_out = (r1 + mixture).astype(BF16)[None]

    out_parts = gather_ctx(grad_out_piece)
    owned_parts = gather_ctx(owned)
    grad_query, grad_key, grad_value, mine = assemble(owned_parts, c_vec, qc, share)
    grad_out = assemble_columns(out_parts, c_vec)
    return (
        block_out,
        grad_in,
        grad_query,
        grad_key,
        grad_value,
        grad_out,
        mine[:, :E],
        mine[:, E],
        mine[:, E + 1],
        mine[:gs, E + 2],
        mine[:gs, E + 3],
        grad_gate[None],
        grad_up[None],
        grad_down[None],
    )


def solution(mesh):
    token = P("shard", "ctx", None)
    row = P("shard", None)
    vector = P("shard")
    expert = P(("ctx", "shard"), None, None)
    return jax.shard_map(
        layer,
        mesh=mesh,
        in_specs=(token, token, token, P())
        + (vector,) * 4
        + (row,) * 5
        + (expert,) * 3,
        out_specs=(token, token) + (row,) * 5 + (vector,) * 4 + (expert,) * 3,
        check_vma=False,
    )
```

```python
import math

import jax
import jax.numpy as jnp
from jax import lax
from jax.experimental import pallas as pl
from jax.experimental.pallas import tpu as pltpu
from jax.sharding import PartitionSpec as P


QUERY_HEADS = 32
KEY_VALUE_HEADS = 4
HEAD_SIZE = 128
TOP = 8

EPS = 1e-06
THETA = 1000000.0
MASKED = -1e30
LANES = 128
VMEM_LIMIT = 58 * 1024 * 1024
F32 = jnp.float32
BF16 = jnp.bfloat16


def dot(a, b, ca=1, cb=0):
    return lax.dot_general(a, b, (((ca,), (cb,)), ((), ())), preferred_element_type=F32)


def params(**kw):
    return pltpu.CompilerParams(vmem_limit_bytes=VMEM_LIMIT, **kw)


def inverse_rms(v):
    return lax.rsqrt(jnp.mean(v * v, axis=-1, keepdims=True) + EPS)


def turn(v, cosine, sine):
    return v * cosine + pltpu.roll(v, HEAD_SIZE // 2, 1) * sine


def head(pre, gain, cosine, sine):
    return turn(pre * inverse_rms(pre) * gain, cosine, sine).astype(BF16)


def head_back(grad, pre, gain, cosine, sine):
    g = turn(grad, cosine, -sine)
    r = inverse_rms(pre)
    n = pre * r
    scaled = g * gain
    back = r * (scaled - n * jnp.mean(n * scaled, axis=-1, keepdims=True))
    return back.astype(BF16), jnp.sum(g * n, axis=0, keepdims=True)


def attend_forward(qkv, heads, gains, cosine, sine, pos_col, pos_row):
    n = qkv.shape[0]
    hs = HEAD_SIZE
    factor = math.log2(math.e) / math.sqrt(HEAD_SIZE)

    def kernel(q_ref, k_ref, v_ref, gain_ref, cos_ref, sin_ref, pc_ref, pr_ref, out_ref, tot_ref, key_s, val_s, bias_s):
        h = pl.program_id(0)

        @pl.when(h == 0)
        def _():
            key_s[...] = head(k_ref[...], gain_ref[1:2, :], cos_ref[...], sin_ref[...])
            val_s[:, :hs] = v_ref[...].astype(BF16)
            val_s[:, hs:] = jnp.ones((n, hs), BF16)
            bias_s[...] = jnp.where(pc_ref[...] >= pr_ref[...], 0.0, MASKED)
            tot_ref[...] = jnp.zeros_like(tot_ref)

        q = head(q_ref[...], gain_ref[0:1, :], cos_ref[...], sin_ref[...])
        e = jnp.exp2(dot(q, key_s[...], 1, 1) * factor + bias_s[...]).astype(BF16)
        both = dot(e, val_s[...])
        inverse = 1.0 / both[:, hs:]
        out_ref[...] = (both[:, :hs] * inverse).astype(BF16)
        lane = lax.broadcasted_iota(jnp.int32, (n, hs), 1)
        tot_ref[...] = jnp.where(lane == h, inverse, tot_ref[...])

    full = lambda a: pl.BlockSpec(a.shape, lambda h: (0, 0))
    return pl.pallas_call(
        kernel,
        grid=(heads,),
        in_specs=[
            pl.BlockSpec((n, hs), lambda h: (0, h)),
            pl.BlockSpec((n, hs), lambda h: (0, heads)),
            pl.BlockSpec((n, hs), lambda h: (0, heads + 1)),
            full(gains),
            full(cosine),
            full(sine),
            full(pos_col),
            full(pos_row),
        ],
        out_specs=[pl.BlockSpec((n, hs), lambda h: (0, h)), pl.BlockSpec((n, hs), lambda h: (0, 0))],
        out_shape=[
            jax.ShapeDtypeStruct((n, heads * hs), BF16),
            jax.ShapeDtypeStruct((n, hs), F32),
        ],
        scratch_shapes=[pltpu.VMEM((n, hs), BF16), pltpu.VMEM((n, 2 * hs), BF16), pltpu.VMEM((n, n), F32)],
        compiler_params=params(),
        name="attend_forward",
    )(qkv, qkv, qkv, gains, cosine, sine, pos_col, pos_row)


def attend_backward(qkv, d_mix, mix, totals, heads, gains, cosine, sine, pos_col, pos_row):
    n = qkv.shape[0]
    hs = HEAD_SIZE
    scale = 1.0 / math.sqrt(HEAD_SIZE)
    factor = math.log2(math.e) / math.sqrt(HEAD_SIZE)

    def kernel(q_ref, k_ref, v_ref, dm_ref, mix_ref, tot_ref, gain_ref, cos_ref, sin_ref, pc_ref, pr_ref, dq_ref, dkv_ref, gg_ref, key_s, val_s, dk_s, dv_s, bias_s):
        h = pl.program_id(0)

        @pl.when(h == 0)
        def _():
            key_s[...] = head(k_ref[...], gain_ref[1:2, :], cos_ref[...], sin_ref[...])
            val_s[...] = v_ref[...].astype(BF16)
            bias_s[...] = jnp.where(pc_ref[...] >= pr_ref[...], 0.0, MASKED)
            dk_s[...] = jnp.zeros_like(dk_s)
            dv_s[...] = jnp.zeros_like(dv_s)
            gg_ref[...] = jnp.zeros_like(gg_ref)

        pre = q_ref[...]
        q = head(pre, gain_ref[0:1, :], cos_ref[...], sin_ref[...])
        dm = dm_ref[...]
        lane = lax.broadcasted_iota(jnp.int32, (n, hs), 1)
        inverse = jnp.sum(jnp.where(lane == h, tot_ref[...], 0.0), axis=-1, keepdims=True)
        centre = jnp.sum(dm.astype(F32) * mix_ref[...].astype(F32), axis=-1, keepdims=True)
        p = jnp.exp2(dot(q, key_s[...], 1, 1) * factor + bias_s[...]) * inverse
        dp = dot(dm, val_s[...], 1, 1)
        ds = (p * (dp - centre)).astype(BF16)
        dq = dot(ds, key_s[...]) * scale
        dk_s[...] += dot(ds, q, 0, 0)
        dv_s[...] += dot(p.astype(BF16), dm, 0, 0)
        back, gg = head_back(dq, pre, gain_ref[0:1, :], cos_ref[...], sin_ref[...])
        dq_ref[...] = back
        gg_ref[0:1, :] += gg

        @pl.when(h == heads - 1)
        def _():
            back, gg = head_back(
                dk_s[...] * scale, k_ref[...], gain_ref[1:2, :], cos_ref[...], sin_ref[...]
            )
            dkv_ref[:, :hs] = back
            dkv_ref[:, hs:] = dv_s[...].astype(BF16)
            gg_ref[1:2, :] = gg

    full = lambda a: pl.BlockSpec(a.shape, lambda h: (0, 0))
    col = pl.BlockSpec((n, hs), lambda h: (0, h))
    return pl.pallas_call(
        kernel,
        grid=(heads,),
        in_specs=[
            col,
            pl.BlockSpec((n, hs), lambda h: (0, heads)),
            pl.BlockSpec((n, hs), lambda h: (0, heads + 1)),
            col,
            col,
            full(totals),
            full(gains),
            full(cosine),
            full(sine),
            full(pos_col),
            full(pos_row),
        ],
        out_specs=[col, pl.BlockSpec((n, 2 * hs), lambda h: (0, 0)), pl.BlockSpec((8, hs), lambda h: (0, 0))],
        out_shape=[
            jax.ShapeDtypeStruct((n, heads * hs), BF16),
            jax.ShapeDtypeStruct((n, 2 * hs), BF16),
            jax.ShapeDtypeStruct((8, hs), F32),
        ],
        scratch_shapes=[
            pltpu.VMEM((n, hs), BF16),
            pltpu.VMEM((n, hs), BF16),
            pltpu.VMEM((n, hs), F32),
            pltpu.VMEM((n, hs), F32),
            pltpu.VMEM((n, n), F32),
        ],
        compiler_params=params(),
        name="attend_backward",
    )(qkv, qkv, qkv, d_mix, mix, totals, gains, cosine, sine, pos_col, pos_row)


def expert_piece(x, cot, router, wg, wu, wd, me, experts, back_extra):
    r, d = x.shape
    f = wg.shape[1]
    extra = cot.shape[1] - d

    def kernel(me_ref, x_ref, cot_ref, router_ref, wg_ref, wu_ref, wd_ref,
               mixed_ref, back_ref, hid_ref, deo_ref, dg_ref, du_ref):
        own = me_ref[0]
        xv = x_ref[...]
        lane = lax.broadcasted_iota(jnp.int32, (r, extra), 1)
        mask = (cot_ref[:, d:].astype(F32) > 0.5) & (lane < experts)
        kept = jnp.where(mask, dot(xv, router_ref[...]), MASKED)
        e = jnp.where(mask, jnp.exp(kept - jnp.max(kept, axis=-1, keepdims=True)), 0.0)
        total = jnp.sum(e, axis=-1, keepdims=True)
        gate = jnp.sum(jnp.where(lane == own, e, 0.0), axis=-1, keepdims=True) / jnp.where(total > 0.0, total, 1.0)
        gp = dot(xv, wg_ref[...])
        up = dot(xv, wu_ref[...])
        sig = jax.nn.sigmoid(gp)
        silu = gp * sig
        hid = (silu * up).astype(BF16)
        hid_ref[...] = hid
        eo = dot(hid, wd_ref[...]).astype(BF16).astype(F32)
        dout = cot_ref[:, :d].astype(F32)
        dgr = jnp.sum(dout * eo, axis=-1, keepdims=True)
        mixed_ref[...] = (gate * eo).astype(BF16)
        deo = (gate * dout).astype(BF16)
        deo_ref[...] = deo
        dh = dot(deo, wd_ref[...], 1, 1)
        dg = (dh * up * sig * (1.0 + gp * (1.0 - sig))).astype(BF16)
        du = (dh * silu).astype(BF16)
        dg_ref[...] = dg
        du_ref[...] = du
        back_ref[:, :d] = (dot(dg, wg_ref[...], 1, 1) + dot(du, wu_ref[...], 1, 1)).astype(BF16)
        lane = lax.broadcasted_iota(jnp.int32, (r, back_extra), 1)
        high = dgr.astype(BF16).astype(F32)
        low = dgr - high
        back_ref[:, d:] = jnp.where(lane == own, high, jnp.where(lane == own + experts, low, 0.0)).astype(BF16)

    vm = pl.BlockSpec(memory_space=pltpu.VMEM)
    return pl.pallas_call(
        kernel,
        in_specs=[pl.BlockSpec(memory_space=pltpu.SMEM)] + [vm] * 6,
        out_specs=[vm] * 6,
        out_shape=[
            jax.ShapeDtypeStruct((r, d), BF16),
            jax.ShapeDtypeStruct((r, d + back_extra), BF16),
            jax.ShapeDtypeStruct((r, f), BF16),
            jax.ShapeDtypeStruct((r, d), BF16),
            jax.ShapeDtypeStruct((r, f), BF16),
            jax.ShapeDtypeStruct((r, f), BF16),
        ],
        compiler_params=params(),
        name="expert_piece",
    )(me, x, cot, router, wg, wu, wd)


def expert_grads(xs, dgs, dus, hids, deos, block=256):
    n = len(xs)
    r, d = xs[0].shape
    f = dgs[0].shape[1]

    def kernel(*refs):
        x, dg, du, hid, deo = (refs[i * n : (i + 1) * n] for i in range(5))
        gg_ref, gu_ref, gd_ref, x_s, deo_s, dg_s, du_s, hid_s = refs[5 * n :]

        @pl.when(pl.program_id(0) == 0)
        def _():
            for i in range(n):
                dg_s[i * r : (i + 1) * r, :] = dg[i][...]
                du_s[i * r : (i + 1) * r, :] = du[i][...]
                x_s[i * r : (i + 1) * r, :] = hid[i][:, :block]
            for j in range(f // block):
                if j:
                    for i in range(n):
                        x_s[i * r : (i + 1) * r, :] = hid[i][:, j * block : (j + 1) * block]
                hid_s[j * block : (j + 1) * block, :] = x_s[...].T

        for i in range(n):
            x_s[i * r : (i + 1) * r, :] = x[i][...]
            deo_s[i * r : (i + 1) * r, :] = deo[i][...]
        xt = x_s[...].T
        gg_ref[...] = dot(xt, dg_s[...])
        gu_ref[...] = dot(xt, du_s[...])
        gd_ref[...] = dot(hid_s[...], deo_s[...])

    part = pl.BlockSpec((r, block), lambda j: (0, j))
    whole = pl.BlockSpec((r, f), lambda j: (0, 0))
    return pl.pallas_call(
        kernel,
        grid=(d // block,),
        in_specs=[part] * n + [whole] * (3 * n) + [part] * n,
        out_specs=[pl.BlockSpec((block, f), lambda j: (j, 0))] * 2
        + [pl.BlockSpec((f, block), lambda j: (0, j))],
        out_shape=[jax.ShapeDtypeStruct((d, f), F32)] * 2
        + [jax.ShapeDtypeStruct((f, d), F32)],
        scratch_shapes=[
            pltpu.VMEM((n * r, block), BF16),
            pltpu.VMEM((n * r, block), BF16),
            pltpu.VMEM((n * r, f), BF16),
            pltpu.VMEM((n * r, f), BF16),
            pltpu.VMEM((f, n * r), BF16),
        ],
        compiler_params=params(),
        name="expert_grads",
    )(*xs, *dgs, *dus, *hids, *deos)


def combine(place, parts, lo, hi, block=512):
    n = len(parts)
    m = place.shape[0]
    r = parts[0].shape[0]
    first = lo // block

    def kernel(place_ref, *refs):
        v, out_ref, v_s = refs[:n], refs[n], refs[n + 1]
        for i in range(n):
            v_s[i * r : (i + 1) * r, :] = v[i][...]
        out_ref[...] = dot(place_ref[...], v_s[...]).astype(BF16)

    return pl.pallas_call(
        kernel,
        grid=(pl.cdiv(hi - lo, block),),
        in_specs=[pl.BlockSpec(place.shape, lambda j: (0, 0))]
        + [pl.BlockSpec((r, block), lambda j: (0, first + j))] * n,
        out_specs=pl.BlockSpec((m, block), lambda j: (0, j)),
        out_shape=jax.ShapeDtypeStruct((m, hi - lo), BF16),
        scratch_shapes=[pltpu.VMEM((n * r, block), BF16)],
        compiler_params=params(),
    )(place, *parts)


def assemble(parts, c, qc, share):
    n = len(parts)
    rows = parts[0].shape[0]
    hs = HEAD_SIZE
    kw = n // share * hs

    def kernel(c_ref, *refs):
        v = refs[:n]
        q_ref, k_ref, v_ref, small_ref = refs[n:]
        small_ref[...] = sum(v[d][:, qc + 2 * hs :].astype(F32) for d in range(n))
        if share > 1:
            k_ref[...] = jnp.zeros_like(k_ref)
            v_ref[...] = jnp.zeros_like(v_ref)
        for d in range(n):
            at = c_ref[0] ^ d
            q_ref[:, pl.ds(pl.multiple_of(at * qc, qc), qc)] = v[d][:, :qc].astype(F32)
            to = pl.ds(pl.multiple_of(at // share * hs, hs), hs)
            key = v[d][:, qc : qc + hs].astype(F32)
            val = v[d][:, qc + hs : qc + 2 * hs].astype(F32)
            if share > 1:
                k_ref[:, to] += key
                v_ref[:, to] += val
            else:
                k_ref[:, to] = key
                v_ref[:, to] = val

    vm = pl.BlockSpec(memory_space=pltpu.VMEM)
    return pl.pallas_call(
        kernel,
        in_specs=[pl.BlockSpec(memory_space=pltpu.SMEM)] + [vm] * n,
        out_specs=[vm] * 4,
        out_shape=[
            jax.ShapeDtypeStruct((rows, n * qc), F32),
            jax.ShapeDtypeStruct((rows, kw), F32),
            jax.ShapeDtypeStruct((rows, kw), F32),
            jax.ShapeDtypeStruct((rows, parts[0].shape[1] - qc - 2 * hs), F32),
        ],
        compiler_params=params(),
        name="assemble",
    )(c, *parts)


def weight_grads(h1, d_q, d_kv, small, block=256):
    n, d = h1.shape
    qc, kc, sc = d_q.shape[1], d_kv.shape[1], small.shape[1]

    def kernel(h_ref, q_ref, kv_ref, small_ref, out_ref):
        h = h_ref[...].T
        out_ref[:, :qc] = dot(h, q_ref[...], 1, 0).astype(BF16)
        out_ref[:, qc : qc + kc] = dot(h, kv_ref[...], 1, 0).astype(BF16)
        out_ref[:, qc + kc :] = small_ref[...]

    return pl.pallas_call(
        kernel,
        grid=(d // block,),
        in_specs=[
            pl.BlockSpec((n, block), lambda j: (0, j)),
            pl.BlockSpec((n, qc), lambda j: (0, 0)),
            pl.BlockSpec((n, kc), lambda j: (0, 0)),
            pl.BlockSpec((block, sc), lambda j: (j, 0)),
        ],
        out_specs=pl.BlockSpec((block, qc + kc + sc), lambda j: (j, 0)),
        out_shape=jax.ShapeDtypeStruct((d, qc + kc + sc), BF16),
        compiler_params=params(),
        name="weight_grads",
    )(h1, d_q, d_kv, small)


def assemble_columns(parts, c):
    n = len(parts)
    rows, w = parts[0].shape

    def kernel(c_ref, *refs):
        for d in range(n):
            at = pl.multiple_of((c_ref[0] ^ d) * w, w)
            refs[n][:, pl.ds(at, w)] = refs[d][...].astype(F32)

    vm = pl.BlockSpec(memory_space=pltpu.VMEM)
    return pl.pallas_call(
        kernel,
        in_specs=[pl.BlockSpec(memory_space=pltpu.SMEM)] + [vm] * n,
        out_specs=vm,
        out_shape=jax.ShapeDtypeStruct((rows, n * w), F32),
        compiler_params=params(),
        name="assemble_columns",
    )(c, *parts)


def plan(targets, rows, block=LANES):
    n, m = targets.shape

    def kernel(row_ref, col_ref, *outs):
        ids = lax.broadcasted_iota(jnp.int32, (rows, block), 0)
        for d in range(n):
            outs[d][...] = jnp.where(row_ref[d : d + 1, :] == ids, 1.0, 0.0).astype(BF16)
        ids = lax.broadcasted_iota(jnp.int32, (block, n * rows), 1)
        hot = col_ref[:, 0:1] == ids
        for d in range(1, n):
            hot = hot | (col_ref[:, d : d + 1] + d * rows == ids)
        outs[n][...] = jnp.where(hot, 1.0, 0.0).astype(BF16)

    return pl.pallas_call(
        kernel,
        grid=(m // block,),
        in_specs=[
            pl.BlockSpec((n, block), lambda j: (0, j)),
            pl.BlockSpec((block, n), lambda j: (j, 0)),
        ],
        out_specs=[pl.BlockSpec((rows, block), lambda j: (0, j))] * n
        + [pl.BlockSpec((block, n * rows), lambda j: (j, 0))],
        out_shape=[jax.ShapeDtypeStruct((rows, m), BF16)] * n
        + [jax.ShapeDtypeStruct((m, n * rows), BF16)],
        compiler_params=params(),
        name="plan",
    )(targets, targets.T)


def norm_rows(parts, gain):
    n = len(parts)
    t, d = parts[0].shape

    def kernel(gain_ref, *refs):
        for i in range(n):
            v = refs[i][...].astype(F32)
            refs[n][i * t : (i + 1) * t, :] = (v * inverse_rms(v) * gain_ref[...]).astype(BF16)

    vm = pl.BlockSpec(memory_space=pltpu.VMEM)
    return pl.pallas_call(
        kernel,
        in_specs=[vm] * (n + 1),
        out_specs=vm,
        out_shape=jax.ShapeDtypeStruct((n * t, d), BF16),
        compiler_params=params(),
        name="norm_rows",
    )(gain, *parts)


def out_proj(parts, w_cols, c):
    n = len(parts)
    t, k = parts[0].shape
    w = w_cols.shape[1]

    def kernel(c_ref, *refs):
        w_ref, out_ref, acc_ref = refs[n:]
        d = pl.program_id(0)
        for i in range(n):

            @pl.when(d == i)
            def _():
                part = dot(refs[i][...], w_ref[...])
                for b in range(n):
                    to, of = b * (t // n), (b ^ i) * (t // n)
                    block = part[of : of + t // n, :]
                    if i == 0:
                        acc_ref[to : to + t // n, :] = block
                    elif i < n - 1:
                        acc_ref[to : to + t // n, :] += block
                    else:
                        total = acc_ref[to : to + t // n, :] + block
                        out_ref[to : to + t // n, :] = total.astype(BF16)

    return pl.pallas_call(
        kernel,
        grid_spec=pltpu.PrefetchScalarGridSpec(
            num_scalar_prefetch=1,
            grid=(n,),
            in_specs=[pl.BlockSpec((t, k), lambda d, c_ref: (0, 0))] * n
            + [pl.BlockSpec((k, w), lambda d, c_ref: (c_ref[0] ^ d, 0))],
            out_specs=pl.BlockSpec((t, w), lambda d, c_ref: (0, 0)),
            scratch_shapes=[pltpu.VMEM((t, w), F32)],
        ),
        out_shape=jax.ShapeDtypeStruct((t, w), BF16),
        compiler_params=params(),
        name="out_proj",
    )(c, *parts, w_cols)


def turn_mixes(mixes, block=512):
    n = len(mixes)
    t, k = mixes[0].shape
    nb = k // block

    def kernel(*refs):
        i = pl.program_id(0)
        for e in range(n):

            @pl.when(i == e)
            def _():
                refs[n][...] = refs[e][...].T

    def pick(e):
        return pl.BlockSpec((t, block), lambda i, j: (0, jnp.where(i < e, 0, jnp.where(i > e, nb - 1, j))))

    return pl.pallas_call(
        kernel,
        grid=(n, nb),
        in_specs=[pick(e) for e in range(n)],
        out_specs=pl.BlockSpec((block, t), lambda i, j: (i * nb + j, 0)),
        out_shape=jax.ShapeDtypeStruct((n * k, t), BF16),
        compiler_params=params(),
        name="turn_mixes",
    )(*mixes)


def out_grads(mix_t, d_parts, c, block=512):
    n = len(d_parts)
    k, t = mix_t.shape[0] // n, mix_t.shape[1]
    rows, d_model = d_parts[0].shape
    w = d_model // n
    nb = k // block

    def kernel(c_ref, m_ref, *refs):
        dp, out_ref, d_s = refs[:n], refs[n], refs[n + 1]
        i, j = pl.program_id(0), pl.program_id(1)

        @pl.when((i == 0) & (j == 0))
        def _():
            for e in range(n):
                for b in range(n):
                    d_s[e, b * rows : (b + 1) * rows, :] = dp[b ^ e][...]

        out_ref[...] = dot(m_ref[...], d_s[i]).astype(BF16)

    return pl.pallas_call(
        kernel,
        grid_spec=pltpu.PrefetchScalarGridSpec(
            num_scalar_prefetch=1,
            grid=(n, nb),
            in_specs=[pl.BlockSpec((block, t), lambda i, j, c_ref: (i * nb + j, 0))]
            + [pl.BlockSpec((rows, w), lambda i, j, c_ref: (0, c_ref[0]))] * n,
            out_specs=pl.BlockSpec((block, w), lambda i, j, c_ref: ((c_ref[0] ^ i) * nb + j, 0)),
            scratch_shapes=[pltpu.VMEM((n, t, w), BF16)],
        ),
        out_shape=jax.ShapeDtypeStruct((n * k, w), BF16),
        compiler_params=params(),
        name="out_grads",
    )(c, mix_t, *d_parts)


def residual(x, parts, gain, c):
    n = len(parts)
    w = parts[0].shape[1]

    def kernel(c_ref, x_ref, gain_ref, *refs):
        r1_ref, h2_ref = refs[n:]
        for i in range(n):
            at = pl.ds(pl.multiple_of((c_ref[0] ^ i) * w, w), w)
            r1_ref[:, at] = x_ref[:, at].astype(F32) + refs[i][...].astype(F32)
        v = r1_ref[...]
        h2_ref[...] = (v * inverse_rms(v) * gain_ref[...]).astype(BF16)

    vm = pl.BlockSpec(memory_space=pltpu.VMEM)
    return pl.pallas_call(
        kernel,
        in_specs=[pl.BlockSpec(memory_space=pltpu.SMEM)] + [vm] * (n + 2),
        out_specs=[vm] * 2,
        out_shape=[jax.ShapeDtypeStruct(x.shape, F32), jax.ShapeDtypeStruct(x.shape, BF16)],
        compiler_params=params(),
        name="residual",
    )(c, x, gain, *parts)


def masked_softmax(logits, mask):
    kept = jnp.where(mask, logits, MASKED)
    e = jnp.where(mask, jnp.exp(kept - jnp.max(kept, axis=-1, keepdims=True)), 0.0)
    total = jnp.sum(e, axis=-1, keepdims=True)
    return e / jnp.where(total > 0.0, total, 1.0)


def norm_back(v, gain, grad):
    r = inverse_rms(v)
    n = v * r
    scaled = grad * gain
    back = r * (scaled - n * jnp.mean(n * scaled, axis=-1, keepdims=True))
    return back, grad * n


def turn_back(back_sum, r1, h2, cot, hits, router, gain, experts):
    t, d = r1.shape
    extra = hits.shape[1]

    def kernel(back_ref, r1_ref, h2_ref, cot_ref, hit_ref, router_ref, gain_ref, dr_ref, da_ref, gr_ref, gn_ref):
        gates = masked_softmax(
            dot(h2_ref[...], router_ref[...]), hit_ref[...].astype(F32) > 0.5
        )
        high = back_ref[:, d : d + extra].astype(F32)
        if experts % LANES:
            d_gates = high + pltpu.roll(high, extra - experts, 1)
        else:
            d_gates = high + back_ref[:, d + experts : d + experts + extra].astype(F32)
        centre = jnp.sum(gates * d_gates, axis=-1, keepdims=True)
        d_logits = (gates * (d_gates - centre)).astype(BF16)
        gr_ref[...] = dot(h2_ref[...], d_logits, 0, 0)
        d_h2 = back_ref[:, :d].astype(F32) + dot(d_logits, router_ref[...], 1, 1)
        back, gain_rows = norm_back(r1_ref[...], gain_ref[...], d_h2)
        gn_ref[...] = jnp.sum(gain_rows, axis=0, keepdims=True)
        total = cot_ref[...].astype(F32) + back
        dr_ref[...] = total
        da_ref[...] = total.astype(BF16)

    vm = pl.BlockSpec(memory_space=pltpu.VMEM)
    return pl.pallas_call(
        kernel,
        in_specs=[vm] * 7,
        out_specs=[vm] * 4,
        out_shape=[
            jax.ShapeDtypeStruct((t, d), F32),
            jax.ShapeDtypeStruct((t, d), BF16),
            jax.ShapeDtypeStruct((d, extra), F32),
            jax.ShapeDtypeStruct((1, d), F32),
        ],
        compiler_params=params(),
        name="turn_back",
    )(back_sum, r1, h2, cot, hits, router, gain)


def input_back(x, parts, d_r1, gain):
    n = len(parts)

    def kernel(x_ref, dr_ref, gain_ref, *refs):
        grad = refs[0][...].astype(F32)
        for i in range(1, n):
            grad = grad + refs[i][...].astype(F32)
        back, _ = norm_back(x_ref[...].astype(F32), gain_ref[...], grad)
        refs[n][...] = dr_ref[...] + back

    vm = pl.BlockSpec(memory_space=pltpu.VMEM)
    return pl.pallas_call(
        kernel,
        in_specs=[vm] * (n + 3),
        out_specs=vm,
        out_shape=jax.ShapeDtypeStruct(x.shape, F32),
        compiler_params=params(),
        name="input_back",
    )(x, d_r1, gain, *parts)


def round_up(n, m):
    return (n + m - 1) // m * m


def rows_of_pair(pair_value, row_count, pair_count):
    row_ids = jnp.arange(row_count, dtype=jnp.int32)
    half = row_count // 2
    block = jnp.where(row_ids >= half, 2 * pair_count - 1 - pair_value, pair_value)
    return block * half + row_ids % half


def layer(
    hidden_in,
    out_cot,
    routes,
    block_pairs,
    norm_attn,
    norm_moe,
    q_gain,
    k_gain,
    w_query,
    w_key,
    w_value,
    w_out,
    w_router,
    expert_gate,
    expert_up,
    expert_down,
):
    C = lax.axis_size("ctx")
    S = lax.axis_size("shard")
    T = hidden_in.shape[1]
    D = hidden_in.shape[2]
    E = C * S
    M = S * T
    QW = QUERY_HEADS * HEAD_SIZE
    qc = QW // C
    share = C // KEY_VALUE_HEADS
    hc = qc // HEAD_SIZE
    cap = max(2, (17 * T * TOP + 16 * E - 1) // (16 * E))
    rows = S * cap
    ws = w_query.shape[0]
    gs = q_gain.shape[0]
    po = QW // E
    c = lax.axis_index("ctx")
    s = lax.axis_index("shard")
    me = c * S + s
    c_vec = c.astype(jnp.int32).reshape(1)

    def exchange_ctx(parts):
        out = [parts[0]]
        for d in range(1, C):
            out.append(lax.ppermute(parts[d], "ctx", [(i, i ^ d) for i in range(C)]))
        return out

    def gather_ctx(v):
        return exchange_ctx([v] * C)

    def gather_shard(v):
        return lax.all_gather(v, "shard", axis=0, tiled=True)

    def sum_shard(v):
        return lax.psum_scatter(v, "shard", scatter_dimension=0, tiled=True)

    kv = c // share
    packed = jnp.concatenate(
        [
            lax.dynamic_slice_in_dim(w_query, c * qc, qc, 1),
            lax.dynamic_slice_in_dim(w_key, kv * HEAD_SIZE, HEAD_SIZE, 1),
            lax.dynamic_slice_in_dim(w_value, kv * HEAD_SIZE, HEAD_SIZE, 1),
        ],
        axis=1,
    )
    w_qkv = gather_shard(packed)
    hits = (
        (routes[0][:, :, None] == jnp.arange(E, dtype=jnp.int32)[None, None, :])
        .any(axis=1)
        .astype(BF16)
    )
    rw = ws * E // T
    nw = ws // T
    small_parts = [
        hits,
        w_router.reshape(T, rw),
        norm_moe.reshape(T, nw),
        norm_attn.reshape(T, nw),
        jnp.pad(jnp.concatenate([q_gain, k_gain]), (0, T - 2 * gs)).reshape(T, 1),
    ]
    small_width = round_up(E + rw + 2 * nw + 1, LANES)
    small_parts.append(jnp.zeros((T, small_width - E - rw - 2 * nw - 1), BF16))
    table = gather_shard(jnp.concatenate(small_parts, axis=1))
    x_own = hidden_in[0]
    x_parts = gather_ctx(x_own)
    hits_column = table[:, :E]
    router = table[:, E : E + rw].reshape(D, E)
    gain_moe = table[:, E + rw : E + rw + nw].reshape(D).astype(F32)
    gain_attn = table[:, E + rw + nw : E + rw + 2 * nw].reshape(D).astype(F32)
    head_gains = table[:, E + rw + 2 * nw].reshape(S, T).astype(F32)
    head_gains = jnp.concatenate(
        [
            head_gains[:, :gs].reshape(1, -1),
            head_gains[:, gs : 2 * gs].reshape(1, -1),
            jnp.zeros((6, HEAD_SIZE), F32),
        ],
        axis=0,
    )

    spread = [((p % C) * S + p // C, p) for p in range(E)]
    piece = lax.ppermute(lax.dynamic_slice_in_dim(w_out, c * po, po, 0), ("ctx", "shard"), spread)
    w_out_rows = gather_shard(piece)
    dc = D // C
    w_out_cols = gather_shard(lax.dynamic_slice_in_dim(w_out, c * dc, dc, 1))

    extra = round_up(E, LANES)
    hits_wide = jnp.pad(hits, ((0, 0), (0, extra - E)))
    cot_own = jnp.concatenate([out_cot[0], hits_wide], axis=1)
    cot_column = gather_shard(cot_own)
    router_wide = jnp.pad(router, ((0, 0), (0, extra - E)))

    pairs_here = jnp.stack([block_pairs[c ^ d] for d in range(C)])
    positions = jax.vmap(lambda p: rows_of_pair(p, T, C))(pairs_here).reshape(-1)
    frequency = THETA ** (-(jnp.arange(HEAD_SIZE // 2, dtype=F32) * 2.0) / HEAD_SIZE)
    phase = positions.astype(F32)[:, None] * frequency[None, :]
    cosine, sine = jnp.cos(phase), jnp.sin(phase)
    cosine = jnp.concatenate([cosine, cosine], axis=1)
    sine = jnp.concatenate([-sine, sine], axis=1)
    pos_col, pos_row = positions[:, None], positions[None, :]

    own_experts = (
        jnp.arange(E, dtype=jnp.int32)[None, :]
        == ((c ^ jnp.arange(C, dtype=jnp.int32)) * S + s)[:, None]
    ).astype(BF16)
    hit = dot(own_experts, hits_column, 1, 1).reshape(C, S, T)
    slot = (jnp.cumsum(hit, axis=2) - hit).astype(jnp.int32)
    target = jnp.where(
        hit > 0.5, jnp.arange(S, dtype=jnp.int32)[None, :, None] * cap + slot, -E * cap
    )
    *picks, place = plan(target.reshape(C, M), rows)

    h1 = norm_rows(x_parts, gain_attn.reshape(1, D))
    qkv = dot(h1, w_qkv, 1, 0)
    mix, totals = attend_forward(qkv, hc, head_gains, cosine, sine, pos_col, pos_row)
    mixes = gather_ctx(mix)
    mix_t = turn_mixes(mixes)
    attn_cols = out_proj(mixes, w_out_cols, c_vec).reshape(C, T, dc)
    attn_out = exchange_ctx([attn_cols[d] for d in range(C)])
    r1, h2 = residual(x_own, attn_out, gain_moe.reshape(1, D), c_vec)

    h2_column = gather_shard(h2)

    def dispatch(v):
        sent = [None] * C
        for d in [C - 1] + list(range(1, C - 1)) + [0]:
            sent[d] = dot(picks[d], v, 1, 0).astype(BF16)
        return exchange_ctx(sent)

    cot_in = dispatch(cot_column)
    expert_in = dispatch(h2_column)

    wg, wu, wd = expert_gate[0], expert_up[0], expert_down[0]
    me_vec = me.astype(jnp.int32).reshape(1)
    back_extra = round_up(2 * E, LANES)
    done = [None] * C
    for d in [0, C - 1] + list(range(1, C - 1)):
        done[d] = expert_piece(
            expert_in[d], cot_in[d], router_wide, wg, wu, wd, me_vec, E, back_extra
        )
    mixed_rows, back_rows, hidden, d_expert_out, d_gate, d_up = (list(v) for v in zip(*done))
    back_in = exchange_ctx(back_rows)
    back_sum = sum_shard(combine(place, back_in, 0, D + back_extra, 768))
    mixed_in = exchange_ctx(mixed_rows)
    grad_gate, grad_up, grad_down = expert_grads(expert_in, d_gate, d_up, hidden, d_expert_out)

    d_r1, d_attn_own, grad_router, grad_norm_moe = turn_back(
        back_sum, r1, h2, out_cot[0], hits_wide, router_wide, gain_moe.reshape(1, D), E
    )
    d_attn_parts = gather_ctx(d_attn_own)
    grad_out_piece = sum_shard(out_grads(mix_t, d_attn_parts, c_vec))
    d_attn = jnp.concatenate(d_attn_parts, axis=0)
    d_mix = dot(d_attn, w_out_rows, 1, 1).astype(BF16)
    d_q, d_kv, gain_grads = attend_backward(
        qkv, d_mix, mix, totals, hc, head_gains, cosine, sine, pos_col, pos_row
    )
    d_qkv = jnp.concatenate([d_q, d_kv], axis=1)

    x_seq = jnp.concatenate(x_parts, axis=0).astype(F32)
    d_h1_partial = dot(d_qkv, w_qkv, 1, 1)
    grad_norm_attn = jnp.sum(d_h1_partial * (x_seq * inverse_rms(x_seq)), axis=0)

    def shard_column(v):
        return jnp.pad(v.reshape(S, gs), ((0, 0), (0, ws - gs))).reshape(-1)

    wide = round_up(E + 4, LANES)
    lane = jnp.arange(wide, dtype=jnp.int32)[None, :]
    small = jnp.pad(grad_router[:, :E], ((0, 0), (0, wide - E)))
    columns = (
        grad_norm_attn,
        grad_norm_moe.reshape(D),
        shard_column(gain_grads[0]),
        shard_column(gain_grads[1]),
    )
    for i, v in enumerate(columns):
        small = small + jnp.where(lane == E + i, v[:, None], 0.0)
    owned_partial = weight_grads(h1, d_q, d_kv, small.astype(BF16))
    owned = sum_shard(owned_partial)

    d_h1_parts = d_h1_partial.astype(BF16).reshape(C, T, D)
    d_h1_in = exchange_ctx([d_h1_parts[d] for d in range(C)])
    grad_in = input_back(x_own, d_h1_in, d_r1, gain_attn.reshape(1, D))[None]

    halves = [sum_shard(combine(place, mixed_in, i * D // 2, (i + 1) * D // 2)) for i in range(2)]
    mixture = jnp.concatenate(halves, axis=1).astype(F32)
    block_out = (r1 + mixture).astype(BF16)[None]

    out_parts = gather_ctx(grad_out_piece)
    owned_parts = gather_ctx(owned)
    grad_query, grad_key, grad_value, mine = assemble(owned_parts, c_vec, qc, share)
    grad_out = assemble_columns(out_parts, c_vec)
    return (
        block_out,
        grad_in,
        grad_query,
        grad_key,
        grad_value,
        grad_out,
        mine[:, :E],
        mine[:, E],
        mine[:, E + 1],
        mine[:gs, E + 2],
        mine[:gs, E + 3],
        grad_gate[None],
        grad_up[None],
        grad_down[None],
    )


def solution(mesh):
    token = P("shard", "ctx", None)
    row = P("shard", None)
    vector = P("shard")
    expert = P(("ctx", "shard"), None, None)
    return jax.shard_map(
        layer,
        mesh=mesh,
        in_specs=(token, token, token, P())
        + (vector,) * 4
        + (row,) * 5
        + (expert,) * 3,
        out_specs=(token, token) + (row,) * 5 + (vector,) * 4 + (expert,) * 3,
        check_vma=False,
    )
```

```python
import math

import jax
import jax.numpy as jnp
from jax import lax
from jax.experimental import pallas as pl
from jax.experimental.pallas import tpu as pltpu
from jax.sharding import PartitionSpec as P


QUERY_HEADS = 32
KEY_VALUE_HEADS = 4
HEAD_SIZE = 128
TOP = 8

EPS = 1e-06
THETA = 1000000.0
MASKED = -1e30
LANES = 128
VMEM_LIMIT = 58 * 1024 * 1024
F32 = jnp.float32
BF16 = jnp.bfloat16


def dot(a, b, ca=1, cb=0):
    return lax.dot_general(a, b, (((ca,), (cb,)), ((), ())), preferred_element_type=F32)


def params(**kw):
    return pltpu.CompilerParams(vmem_limit_bytes=VMEM_LIMIT, **kw)


def inverse_rms(v):
    return lax.rsqrt(jnp.mean(v * v, axis=-1, keepdims=True) + EPS)


def turn(v, cosine, sine):
    return v * cosine + pltpu.roll(v, HEAD_SIZE // 2, 1) * sine


def head(pre, gain, cosine, sine):
    return turn(pre * inverse_rms(pre) * gain, cosine, sine).astype(BF16)


def head_back(grad, pre, gain, cosine, sine):
    g = turn(grad, cosine, -sine)
    r = inverse_rms(pre)
    n = pre * r
    scaled = g * gain
    back = r * (scaled - n * jnp.mean(n * scaled, axis=-1, keepdims=True))
    return back.astype(BF16), jnp.sum(g * n, axis=0, keepdims=True)


def attend_forward(qkv, heads, gains, cosine, sine, pos_col, pos_row):
    n = qkv.shape[0]
    hs = HEAD_SIZE
    factor = math.log2(math.e) / math.sqrt(HEAD_SIZE)

    def kernel(q_ref, k_ref, v_ref, gain_ref, cos_ref, sin_ref, pc_ref, pr_ref, out_ref, tot_ref, key_s, val_s, bias_s):
        h = pl.program_id(0)

        @pl.when(h == 0)
        def _():
            key_s[...] = head(k_ref[...], gain_ref[1:2, :], cos_ref[...], sin_ref[...])
            val_s[:, :hs] = v_ref[...].astype(BF16)
            val_s[:, hs:] = jnp.ones((n, hs), BF16)
            bias_s[...] = jnp.where(pc_ref[...] >= pr_ref[...], 0.0, MASKED)
            tot_ref[...] = jnp.zeros_like(tot_ref)

        q = head(q_ref[...], gain_ref[0:1, :], cos_ref[...], sin_ref[...])
        e = jnp.exp2(dot(q, key_s[...], 1, 1) * factor + bias_s[...]).astype(BF16)
        both = dot(e, val_s[...])
        inverse = 1.0 / both[:, hs:]
        out_ref[...] = (both[:, :hs] * inverse).astype(BF16)
        lane = lax.broadcasted_iota(jnp.int32, (n, hs), 1)
        tot_ref[...] = jnp.where(lane == h, inverse, tot_ref[...])

    full = lambda a: pl.BlockSpec(a.shape, lambda h: (0, 0))
    return pl.pallas_call(
        kernel,
        grid=(heads,),
        in_specs=[
            pl.BlockSpec((n, hs), lambda h: (0, h)),
            pl.BlockSpec((n, hs), lambda h: (0, heads)),
            pl.BlockSpec((n, hs), lambda h: (0, heads + 1)),
            full(gains),
            full(cosine),
            full(sine),
            full(pos_col),
            full(pos_row),
        ],
        out_specs=[pl.BlockSpec((n, hs), lambda h: (0, h)), pl.BlockSpec((n, hs), lambda h: (0, 0))],
        out_shape=[
            jax.ShapeDtypeStruct((n, heads * hs), BF16),
            jax.ShapeDtypeStruct((n, hs), F32),
        ],
        scratch_shapes=[pltpu.VMEM((n, hs), BF16), pltpu.VMEM((n, 2 * hs), BF16), pltpu.VMEM((n, n), F32)],
        compiler_params=params(),
        name="attend",
    )(qkv, qkv, qkv, gains, cosine, sine, pos_col, pos_row)


def attend_backward(qkv, d_mix, mix, totals, heads, gains, cosine, sine, pos_col, pos_row):
    n = qkv.shape[0]
    hs = HEAD_SIZE
    scale = 1.0 / math.sqrt(HEAD_SIZE)
    factor = math.log2(math.e) / math.sqrt(HEAD_SIZE)

    def kernel(q_ref, k_ref, v_ref, dm_ref, mix_ref, tot_ref, gain_ref, cos_ref, sin_ref, pc_ref, pr_ref, dq_ref, dkv_ref, gg_ref, key_s, val_s, dk_s, dv_s, bias_s):
        h = pl.program_id(0)

        @pl.when(h == 0)
        def _():
            key_s[...] = head(k_ref[...], gain_ref[1:2, :], cos_ref[...], sin_ref[...])
            val_s[...] = v_ref[...].astype(BF16)
            bias_s[...] = jnp.where(pc_ref[...] >= pr_ref[...], 0.0, MASKED)
            dk_s[...] = jnp.zeros_like(dk_s)
            dv_s[...] = jnp.zeros_like(dv_s)
            gg_ref[...] = jnp.zeros_like(gg_ref)

        pre = q_ref[...]
        q = head(pre, gain_ref[0:1, :], cos_ref[...], sin_ref[...])
        dm = dm_ref[...]
        lane = lax.broadcasted_iota(jnp.int32, (n, hs), 1)
        inverse = jnp.sum(jnp.where(lane == h, tot_ref[...], 0.0), axis=-1, keepdims=True)
        centre = jnp.sum(dm.astype(F32) * mix_ref[...].astype(F32), axis=-1, keepdims=True)
        p = jnp.exp2(dot(q, key_s[...], 1, 1) * factor + bias_s[...]) * inverse
        dp = dot(dm, val_s[...], 1, 1)
        ds = (p * (dp - centre)).astype(BF16)
        dq = dot(ds, key_s[...]) * scale
        dk_s[...] += dot(ds, q, 0, 0)
        dv_s[...] += dot(p.astype(BF16), dm, 0, 0)
        back, gg = head_back(dq, pre, gain_ref[0:1, :], cos_ref[...], sin_ref[...])
        dq_ref[...] = back
        gg_ref[0:1, :] += gg

        @pl.when(h == heads - 1)
        def _():
            back, gg = head_back(
                dk_s[...] * scale, k_ref[...], gain_ref[1:2, :], cos_ref[...], sin_ref[...]
            )
            dkv_ref[:, :hs] = back
            dkv_ref[:, hs:] = dv_s[...].astype(BF16)
            gg_ref[1:2, :] = gg

    full = lambda a: pl.BlockSpec(a.shape, lambda h: (0, 0))
    col = pl.BlockSpec((n, hs), lambda h: (0, h))
    return pl.pallas_call(
        kernel,
        grid=(heads,),
        in_specs=[
            col,
            pl.BlockSpec((n, hs), lambda h: (0, heads)),
            pl.BlockSpec((n, hs), lambda h: (0, heads + 1)),
            col,
            col,
            full(totals),
            full(gains),
            full(cosine),
            full(sine),
            full(pos_col),
            full(pos_row),
        ],
        out_specs=[col, pl.BlockSpec((n, 2 * hs), lambda h: (0, 0)), pl.BlockSpec((8, hs), lambda h: (0, 0))],
        out_shape=[
            jax.ShapeDtypeStruct((n, heads * hs), BF16),
            jax.ShapeDtypeStruct((n, 2 * hs), BF16),
            jax.ShapeDtypeStruct((8, hs), F32),
        ],
        scratch_shapes=[
            pltpu.VMEM((n, hs), BF16),
            pltpu.VMEM((n, hs), BF16),
            pltpu.VMEM((n, hs), F32),
            pltpu.VMEM((n, hs), F32),
            pltpu.VMEM((n, n), F32),
        ],
        compiler_params=params(),
        name="unattend",
    )(qkv, qkv, qkv, d_mix, mix, totals, gains, cosine, sine, pos_col, pos_row)


def expert_piece(x, cot, router, wg, wu, wd, me, experts, back_extra):
    r, d = x.shape
    f = wg.shape[1]
    extra = cot.shape[1] - d

    def kernel(me_ref, x_ref, cot_ref, router_ref, wg_ref, wu_ref, wd_ref,
               mixed_ref, back_ref, hid_ref, deo_ref, dg_ref, du_ref):
        own = me_ref[0]
        xv = x_ref[...]
        lane = lax.broadcasted_iota(jnp.int32, (r, extra), 1)
        mask = (cot_ref[:, d:].astype(F32) > 0.5) & (lane < experts)
        kept = jnp.where(mask, dot(xv, router_ref[...]), MASKED)
        e = jnp.where(mask, jnp.exp(kept - jnp.max(kept, axis=-1, keepdims=True)), 0.0)
        total = jnp.sum(e, axis=-1, keepdims=True)
        gate = jnp.sum(jnp.where(lane == own, e, 0.0), axis=-1, keepdims=True) / jnp.where(total > 0.0, total, 1.0)
        gp = dot(xv, wg_ref[...])
        up = dot(xv, wu_ref[...])
        sig = jax.nn.sigmoid(gp)
        silu = gp * sig
        hid = (silu * up).astype(BF16)
        hid_ref[...] = hid
        eo = dot(hid, wd_ref[...]).astype(BF16).astype(F32)
        dout = cot_ref[:, :d].astype(F32)
        dgr = jnp.sum(dout * eo, axis=-1, keepdims=True)
        mixed_ref[...] = (gate * eo).astype(BF16)
        deo = (gate * dout).astype(BF16)
        deo_ref[...] = deo
        dh = dot(deo, wd_ref[...], 1, 1)
        dg = (dh * up * sig * (1.0 + gp * (1.0 - sig))).astype(BF16)
        du = (dh * silu).astype(BF16)
        dg_ref[...] = dg
        du_ref[...] = du
        back_ref[:, :d] = (dot(dg, wg_ref[...], 1, 1) + dot(du, wu_ref[...], 1, 1)).astype(BF16)
        lane = lax.broadcasted_iota(jnp.int32, (r, back_extra), 1)
        high = dgr.astype(BF16).astype(F32)
        low = dgr - high
        back_ref[:, d:] = jnp.where(lane == own, high, jnp.where(lane == own + experts, low, 0.0)).astype(BF16)

    vm = pl.BlockSpec(memory_space=pltpu.VMEM)
    return pl.pallas_call(
        kernel,
        in_specs=[pl.BlockSpec(memory_space=pltpu.SMEM)] + [vm] * 6,
        out_specs=[vm] * 6,
        out_shape=[
            jax.ShapeDtypeStruct((r, d), BF16),
            jax.ShapeDtypeStruct((r, d + back_extra), BF16),
            jax.ShapeDtypeStruct((r, f), BF16),
            jax.ShapeDtypeStruct((r, d), BF16),
            jax.ShapeDtypeStruct((r, f), BF16),
            jax.ShapeDtypeStruct((r, f), BF16),
        ],
        compiler_params=params(),
        name="expert_piece",
    )(me, x, cot, router, wg, wu, wd)


def expert_grads(xs, dgs, dus, hids, deos, block=256):
    n = len(xs)
    r, d = xs[0].shape
    f = dgs[0].shape[1]

    def kernel(*refs):
        x, dg, du, hid, deo = (refs[i * n : (i + 1) * n] for i in range(5))
        gg_ref, gu_ref, gd_ref, x_s, deo_s, dg_s, du_s, hid_s = refs[5 * n :]

        @pl.when(pl.program_id(0) == 0)
        def _():
            for i in range(n):
                dg_s[i * r : (i + 1) * r, :] = dg[i][...]
                du_s[i * r : (i + 1) * r, :] = du[i][...]
                x_s[i * r : (i + 1) * r, :] = hid[i][:, :block]
            for j in range(f // block):
                if j:
                    for i in range(n):
                        x_s[i * r : (i + 1) * r, :] = hid[i][:, j * block : (j + 1) * block]
                hid_s[j * block : (j + 1) * block, :] = x_s[...].T

        for i in range(n):
            x_s[i * r : (i + 1) * r, :] = x[i][...]
            deo_s[i * r : (i + 1) * r, :] = deo[i][...]
        xt = x_s[...].T
        gg_ref[...] = dot(xt, dg_s[...])
        gu_ref[...] = dot(xt, du_s[...])
        gd_ref[...] = dot(hid_s[...], deo_s[...])

    part = pl.BlockSpec((r, block), lambda j: (0, j))
    whole = pl.BlockSpec((r, f), lambda j: (0, 0))
    return pl.pallas_call(
        kernel,
        grid=(d // block,),
        in_specs=[part] * n + [whole] * (3 * n) + [part] * n,
        out_specs=[pl.BlockSpec((block, f), lambda j: (j, 0))] * 2
        + [pl.BlockSpec((f, block), lambda j: (0, j))],
        out_shape=[jax.ShapeDtypeStruct((d, f), F32)] * 2
        + [jax.ShapeDtypeStruct((f, d), F32)],
        scratch_shapes=[
            pltpu.VMEM((n * r, block), BF16),
            pltpu.VMEM((n * r, block), BF16),
            pltpu.VMEM((n * r, f), BF16),
            pltpu.VMEM((n * r, f), BF16),
            pltpu.VMEM((f, n * r), BF16),
        ],
        compiler_params=params(),
        name="exgrads",
    )(*xs, *dgs, *dus, *hids, *deos)


def combine(place, parts, lo, hi, block=512):
    n = len(parts)
    m = place.shape[0]
    r = parts[0].shape[0]
    first = lo // block

    def kernel(place_ref, *refs):
        v, out_ref, v_s = refs[:n], refs[n], refs[n + 1]
        for i in range(n):
            v_s[i * r : (i + 1) * r, :] = v[i][...]
        out_ref[...] = dot(place_ref[...], v_s[...]).astype(BF16)

    return pl.pallas_call(
        kernel,
        grid=(pl.cdiv(hi - lo, block),),
        in_specs=[pl.BlockSpec(place.shape, lambda j: (0, 0))]
        + [pl.BlockSpec((r, block), lambda j: (0, first + j))] * n,
        out_specs=pl.BlockSpec((m, block), lambda j: (0, j)),
        out_shape=jax.ShapeDtypeStruct((m, hi - lo), BF16),
        scratch_shapes=[pltpu.VMEM((n * r, block), BF16)],
        compiler_params=params(),
    )(place, *parts)


def assemble(parts, c, qc, share):
    n = len(parts)
    rows = parts[0].shape[0]
    hs = HEAD_SIZE
    kw = n // share * hs

    def kernel(c_ref, *refs):
        v = refs[:n]
        q_ref, k_ref, v_ref, small_ref = refs[n:]
        small_ref[...] = sum(v[d][:, qc + 2 * hs :].astype(F32) for d in range(n))
        if share > 1:
            k_ref[...] = jnp.zeros_like(k_ref)
            v_ref[...] = jnp.zeros_like(v_ref)
        for d in range(n):
            at = c_ref[0] ^ d
            q_ref[:, pl.ds(pl.multiple_of(at * qc, qc), qc)] = v[d][:, :qc].astype(F32)
            to = pl.ds(pl.multiple_of(at // share * hs, hs), hs)
            key = v[d][:, qc : qc + hs].astype(F32)
            val = v[d][:, qc + hs : qc + 2 * hs].astype(F32)
            if share > 1:
                k_ref[:, to] += key
                v_ref[:, to] += val
            else:
                k_ref[:, to] = key
                v_ref[:, to] = val

    vm = pl.BlockSpec(memory_space=pltpu.VMEM)
    return pl.pallas_call(
        kernel,
        in_specs=[pl.BlockSpec(memory_space=pltpu.SMEM)] + [vm] * n,
        out_specs=[vm] * 4,
        out_shape=[
            jax.ShapeDtypeStruct((rows, n * qc), F32),
            jax.ShapeDtypeStruct((rows, kw), F32),
            jax.ShapeDtypeStruct((rows, kw), F32),
            jax.ShapeDtypeStruct((rows, parts[0].shape[1] - qc - 2 * hs), F32),
        ],
        compiler_params=params(),
        name="assemble",
    )(c, *parts)


def weight_grads(h1, d_q, d_kv, small, block=256):
    n, d = h1.shape
    qc, kc, sc = d_q.shape[1], d_kv.shape[1], small.shape[1]

    def kernel(h_ref, q_ref, kv_ref, small_ref, out_ref):
        h = h_ref[...].T
        out_ref[:, :qc] = dot(h, q_ref[...], 1, 0).astype(BF16)
        out_ref[:, qc : qc + kc] = dot(h, kv_ref[...], 1, 0).astype(BF16)
        out_ref[:, qc + kc :] = small_ref[...]

    return pl.pallas_call(
        kernel,
        grid=(d // block,),
        in_specs=[
            pl.BlockSpec((n, block), lambda j: (0, j)),
            pl.BlockSpec((n, qc), lambda j: (0, 0)),
            pl.BlockSpec((n, kc), lambda j: (0, 0)),
            pl.BlockSpec((block, sc), lambda j: (j, 0)),
        ],
        out_specs=pl.BlockSpec((block, qc + kc + sc), lambda j: (j, 0)),
        out_shape=jax.ShapeDtypeStruct((d, qc + kc + sc), BF16),
        compiler_params=params(),
        name="wgrads",
    )(h1, d_q, d_kv, small)


def assemble_columns(parts, c):
    n = len(parts)
    rows, w = parts[0].shape

    def kernel(c_ref, *refs):
        for d in range(n):
            at = pl.multiple_of((c_ref[0] ^ d) * w, w)
            refs[n][:, pl.ds(at, w)] = refs[d][...].astype(F32)

    vm = pl.BlockSpec(memory_space=pltpu.VMEM)
    return pl.pallas_call(
        kernel,
        in_specs=[pl.BlockSpec(memory_space=pltpu.SMEM)] + [vm] * n,
        out_specs=vm,
        out_shape=jax.ShapeDtypeStruct((rows, n * w), F32),
        compiler_params=params(),
        name="columns",
    )(c, *parts)


def pack(w_query, w_key, w_value, at, qc):
    ws = w_query.shape[0]
    hs = HEAD_SIZE

    def kernel(at_ref, q_ref, k_ref, v_ref, out_ref):
        out_ref[:, :qc] = q_ref[...]
        out_ref[:, qc : qc + hs] = k_ref[...]
        out_ref[:, qc + hs :] = v_ref[...]

    head_spec = pl.BlockSpec((ws, hs), lambda j, at_ref: (0, at_ref[1]))
    return pl.pallas_call(
        kernel,
        grid_spec=pltpu.PrefetchScalarGridSpec(
            num_scalar_prefetch=1,
            grid=(1,),
            in_specs=[
                pl.BlockSpec((ws, qc), lambda j, at_ref: (0, at_ref[0])),
                head_spec,
                head_spec,
            ],
            out_specs=pl.BlockSpec((ws, qc + 2 * hs), lambda j, at_ref: (0, 0)),
        ),
        out_shape=jax.ShapeDtypeStruct((ws, qc + 2 * hs), BF16),
        compiler_params=params(),
        name="pack",
    )(at, w_query, w_key, w_value)


def plan(targets, rows, block=LANES):
    n, m = targets.shape

    def kernel(row_ref, col_ref, *outs):
        ids = lax.broadcasted_iota(jnp.int32, (rows, block), 0)
        for d in range(n):
            outs[d][...] = jnp.where(row_ref[d : d + 1, :] == ids, 1.0, 0.0).astype(BF16)
        ids = lax.broadcasted_iota(jnp.int32, (block, n * rows), 1)
        hot = col_ref[:, 0:1] == ids
        for d in range(1, n):
            hot = hot | (col_ref[:, d : d + 1] + d * rows == ids)
        outs[n][...] = jnp.where(hot, 1.0, 0.0).astype(BF16)

    return pl.pallas_call(
        kernel,
        grid=(m // block,),
        in_specs=[
            pl.BlockSpec((n, block), lambda j: (0, j)),
            pl.BlockSpec((block, n), lambda j: (j, 0)),
        ],
        out_specs=[pl.BlockSpec((rows, block), lambda j: (0, j))] * n
        + [pl.BlockSpec((block, n * rows), lambda j: (j, 0))],
        out_shape=[jax.ShapeDtypeStruct((rows, m), BF16)] * n
        + [jax.ShapeDtypeStruct((m, n * rows), BF16)],
        compiler_params=params(),
        name="plan",
    )(targets, targets.T)


def norm_rows(parts, gain):
    n = len(parts)
    t, d = parts[0].shape

    def kernel(gain_ref, *refs):
        for i in range(n):
            v = refs[i][...].astype(F32)
            refs[n][i * t : (i + 1) * t, :] = (v * inverse_rms(v) * gain_ref[...]).astype(BF16)

    vm = pl.BlockSpec(memory_space=pltpu.VMEM)
    return pl.pallas_call(
        kernel,
        in_specs=[vm] * (n + 1),
        out_specs=vm,
        out_shape=jax.ShapeDtypeStruct((n * t, d), BF16),
        compiler_params=params(),
        name="norm_rows",
    )(gain, *parts)


def out_proj(parts, w_cols, c):
    n = len(parts)
    t, k = parts[0].shape
    w = w_cols.shape[1]

    def kernel(c_ref, *refs):
        w_ref, out_ref, acc_ref = refs[n:]
        d = pl.program_id(0)
        for i in range(n):

            @pl.when(d == i)
            def _():
                part = dot(refs[i][...], w_ref[...])
                for b in range(n):
                    to, of = b * (t // n), (b ^ i) * (t // n)
                    block = part[of : of + t // n, :]
                    if i == 0:
                        acc_ref[to : to + t // n, :] = block
                    elif i < n - 1:
                        acc_ref[to : to + t // n, :] += block
                    else:
                        total = acc_ref[to : to + t // n, :] + block
                        out_ref[to : to + t // n, :] = total.astype(BF16)

    return pl.pallas_call(
        kernel,
        grid_spec=pltpu.PrefetchScalarGridSpec(
            num_scalar_prefetch=1,
            grid=(n,),
            in_specs=[pl.BlockSpec((t, k), lambda d, c_ref: (0, 0))] * n
            + [pl.BlockSpec((k, w), lambda d, c_ref: (c_ref[0] ^ d, 0))],
            out_specs=pl.BlockSpec((t, w), lambda d, c_ref: (0, 0)),
            scratch_shapes=[pltpu.VMEM((t, w), F32)],
        ),
        out_shape=jax.ShapeDtypeStruct((t, w), BF16),
        compiler_params=params(),
        name="out_proj",
    )(c, *parts, w_cols)


def turn_mixes(mixes, block=512):
    n = len(mixes)
    t, k = mixes[0].shape
    nb = k // block

    def kernel(*refs):
        i = pl.program_id(0)
        for e in range(n):

            @pl.when(i == e)
            def _():
                refs[n][...] = refs[e][...].T

    def pick(e):
        return pl.BlockSpec((t, block), lambda i, j: (0, jnp.where(i < e, 0, jnp.where(i > e, nb - 1, j))))

    return pl.pallas_call(
        kernel,
        grid=(n, nb),
        in_specs=[pick(e) for e in range(n)],
        out_specs=pl.BlockSpec((block, t), lambda i, j: (i * nb + j, 0)),
        out_shape=jax.ShapeDtypeStruct((n * k, t), BF16),
        compiler_params=params(),
        name="turn",
    )(*mixes)


def out_grads(mix_t, d_parts, c, block=512):
    n = len(d_parts)
    k, t = mix_t.shape[0] // n, mix_t.shape[1]
    rows, d_model = d_parts[0].shape
    w = d_model // n
    nb = k // block

    def kernel(c_ref, m_ref, *refs):
        dp, out_ref, d_s = refs[:n], refs[n], refs[n + 1]
        i, j = pl.program_id(0), pl.program_id(1)

        @pl.when((i == 0) & (j == 0))
        def _():
            for e in range(n):
                for b in range(n):
                    d_s[e, b * rows : (b + 1) * rows, :] = dp[b ^ e][...]

        out_ref[...] = dot(m_ref[...], d_s[i]).astype(BF16)

    return pl.pallas_call(
        kernel,
        grid_spec=pltpu.PrefetchScalarGridSpec(
            num_scalar_prefetch=1,
            grid=(n, nb),
            in_specs=[pl.BlockSpec((block, t), lambda i, j, c_ref: (i * nb + j, 0))]
            + [pl.BlockSpec((rows, w), lambda i, j, c_ref: (0, c_ref[0]))] * n,
            out_specs=pl.BlockSpec((block, w), lambda i, j, c_ref: ((c_ref[0] ^ i) * nb + j, 0)),
            scratch_shapes=[pltpu.VMEM((n, t, w), BF16)],
        ),
        out_shape=jax.ShapeDtypeStruct((n * k, w), BF16),
        compiler_params=params(),
        name="out_grads",
    )(c, mix_t, *d_parts)


def residual(x, parts, gain, c):
    n = len(parts)
    w = parts[0].shape[1]

    def kernel(c_ref, x_ref, gain_ref, *refs):
        r1_ref, h2_ref = refs[n:]
        for i in range(n):
            at = pl.ds(pl.multiple_of((c_ref[0] ^ i) * w, w), w)
            r1_ref[:, at] = x_ref[:, at].astype(F32) + refs[i][...].astype(F32)
        v = r1_ref[...]
        h2_ref[...] = (v * inverse_rms(v) * gain_ref[...]).astype(BF16)

    vm = pl.BlockSpec(memory_space=pltpu.VMEM)
    return pl.pallas_call(
        kernel,
        in_specs=[pl.BlockSpec(memory_space=pltpu.SMEM)] + [vm] * (n + 2),
        out_specs=[vm] * 2,
        out_shape=[jax.ShapeDtypeStruct(x.shape, F32), jax.ShapeDtypeStruct(x.shape, BF16)],
        compiler_params=params(),
        name="residual",
    )(c, x, gain, *parts)


def masked_softmax(logits, mask):
    kept = jnp.where(mask, logits, MASKED)
    e = jnp.where(mask, jnp.exp(kept - jnp.max(kept, axis=-1, keepdims=True)), 0.0)
    total = jnp.sum(e, axis=-1, keepdims=True)
    return e / jnp.where(total > 0.0, total, 1.0)


def norm_back(v, gain, grad):
    r = inverse_rms(v)
    n = v * r
    scaled = grad * gain
    back = r * (scaled - n * jnp.mean(n * scaled, axis=-1, keepdims=True))
    return back, grad * n


def turn_back(back_sum, r1, h2, cot, hits, router, gain, experts):
    t, d = r1.shape
    extra = hits.shape[1]

    def kernel(back_ref, r1_ref, h2_ref, cot_ref, hit_ref, router_ref, gain_ref, dr_ref, da_ref, gr_ref, gn_ref):
        gates = masked_softmax(
            dot(h2_ref[...], router_ref[...]), hit_ref[...].astype(F32) > 0.5
        )
        high = back_ref[:, d : d + extra].astype(F32)
        if experts % LANES:
            d_gates = high + pltpu.roll(high, extra - experts, 1)
        else:
            d_gates = high + back_ref[:, d + experts : d + experts + extra].astype(F32)
        centre = jnp.sum(gates * d_gates, axis=-1, keepdims=True)
        d_logits = (gates * (d_gates - centre)).astype(BF16)
        gr_ref[...] = dot(h2_ref[...], d_logits, 0, 0)
        d_h2 = back_ref[:, :d].astype(F32) + dot(d_logits, router_ref[...], 1, 1)
        back, gain_rows = norm_back(r1_ref[...], gain_ref[...], d_h2)
        gn_ref[...] = jnp.sum(gain_rows, axis=0, keepdims=True)
        total = cot_ref[...].astype(F32) + back
        dr_ref[...] = total
        da_ref[...] = total.astype(BF16)

    vm = pl.BlockSpec(memory_space=pltpu.VMEM)
    return pl.pallas_call(
        kernel,
        in_specs=[vm] * 7,
        out_specs=[vm] * 4,
        out_shape=[
            jax.ShapeDtypeStruct((t, d), F32),
            jax.ShapeDtypeStruct((t, d), BF16),
            jax.ShapeDtypeStruct((d, extra), F32),
            jax.ShapeDtypeStruct((1, d), F32),
        ],
        compiler_params=params(),
        name="turn_back",
    )(back_sum, r1, h2, cot, hits, router, gain)


def input_back(x, parts, d_r1, gain):
    n = len(parts)

    def kernel(x_ref, dr_ref, gain_ref, *refs):
        grad = refs[0][...].astype(F32)
        for i in range(1, n):
            grad = grad + refs[i][...].astype(F32)
        back, _ = norm_back(x_ref[...].astype(F32), gain_ref[...], grad)
        refs[n][...] = dr_ref[...] + back

    vm = pl.BlockSpec(memory_space=pltpu.VMEM)
    return pl.pallas_call(
        kernel,
        in_specs=[vm] * (n + 3),
        out_specs=vm,
        out_shape=jax.ShapeDtypeStruct(x.shape, F32),
        compiler_params=params(),
        name="inback",
    )(x, d_r1, gain, *parts)


def round_up(n, m):
    return (n + m - 1) // m * m


def rows_of_pair(pair_value, row_count, pair_count):
    row_ids = jnp.arange(row_count, dtype=jnp.int32)
    half = row_count // 2
    block = jnp.where(row_ids >= half, 2 * pair_count - 1 - pair_value, pair_value)
    return block * half + row_ids % half


def layer(
    hidden_in,
    out_cot,
    routes,
    block_pairs,
    norm_attn,
    norm_moe,
    q_gain,
    k_gain,
    w_query,
    w_key,
    w_value,
    w_out,
    w_router,
    expert_gate,
    expert_up,
    expert_down,
):
    C = lax.axis_size("ctx")
    S = lax.axis_size("shard")
    T = hidden_in.shape[1]
    D = hidden_in.shape[2]
    E = C * S
    M = S * T
    QW = QUERY_HEADS * HEAD_SIZE
    qc = QW // C
    share = C // KEY_VALUE_HEADS
    hc = qc // HEAD_SIZE
    cap = max(2, (17 * T * TOP + 16 * E - 1) // (16 * E))
    rows = S * cap
    ws = w_query.shape[0]
    gs = q_gain.shape[0]
    po = QW // E
    c = lax.axis_index("ctx")
    s = lax.axis_index("shard")
    me = c * S + s
    c_vec = c.astype(jnp.int32).reshape(1)

    def exchange_ctx(parts):
        out = [parts[0]]
        for d in range(1, C):
            out.append(lax.ppermute(parts[d], "ctx", [(i, i ^ d) for i in range(C)]))
        return out

    def gather_ctx(v):
        return exchange_ctx([v] * C)

    def gather_shard(v):
        return lax.all_gather(v, "shard", axis=0, tiled=True)

    def sum_shard(v):
        return lax.psum_scatter(v, "shard", scatter_dimension=0, tiled=True)

    at = jnp.stack([c, c // share]).astype(jnp.int32)
    packed = pack(w_query, w_key, w_value, at, qc)
    w_qkv = gather_shard(packed)
    hits = (
        (routes[0][:, :, None] == jnp.arange(E, dtype=jnp.int32)[None, None, :])
        .any(axis=1)
        .astype(BF16)
    )
    rw = ws * E // T
    nw = ws // T
    small_parts = [
        hits,
        w_router.reshape(T, rw),
        norm_moe.reshape(T, nw),
        norm_attn.reshape(T, nw),
        jnp.pad(jnp.concatenate([q_gain, k_gain]), (0, T - 2 * gs)).reshape(T, 1),
    ]
    small_width = round_up(E + rw + 2 * nw + 1, LANES)
    small_parts.append(jnp.zeros((T, small_width - E - rw - 2 * nw - 1), BF16))
    table = gather_shard(jnp.concatenate(small_parts, axis=1))
    x_own = hidden_in[0]
    x_parts = gather_ctx(x_own)
    hits_column = table[:, :E]
    router = table[:, E : E + rw].reshape(D, E)
    gain_moe = table[:, E + rw : E + rw + nw].reshape(D).astype(F32)
    gain_attn = table[:, E + rw + nw : E + rw + 2 * nw].reshape(D).astype(F32)
    head_gains = table[:, E + rw + 2 * nw].reshape(S, T).astype(F32)
    head_gains = jnp.concatenate(
        [
            head_gains[:, :gs].reshape(1, -1),
            head_gains[:, gs : 2 * gs].reshape(1, -1),
            jnp.zeros((6, HEAD_SIZE), F32),
        ],
        axis=0,
    )

    pieces = []
    for i in range(C):
        pairs = [(p // S * S + p // C, p) for p in range(E) if p % C == i]
        pieces.append(lax.ppermute(w_out[i * po : (i + 1) * po], ("ctx", "shard"), pairs))
    piece = sum(pieces[1:], pieces[0])
    w_out_rows = gather_shard(piece)
    dc = D // C
    w_out_cols = gather_shard(lax.dynamic_slice_in_dim(w_out, c * dc, dc, 1))

    extra = round_up(E, LANES)
    hits_wide = jnp.pad(hits, ((0, 0), (0, extra - E)))
    cot_own = jnp.concatenate([out_cot[0], hits_wide], axis=1)
    cot_column = gather_shard(cot_own)
    router_wide = jnp.pad(router, ((0, 0), (0, extra - E)))

    pairs_here = jnp.stack([block_pairs[c ^ d] for d in range(C)])
    positions = jax.vmap(lambda p: rows_of_pair(p, T, C))(pairs_here).reshape(-1)
    frequency = THETA ** (-(jnp.arange(HEAD_SIZE // 2, dtype=F32) * 2.0) / HEAD_SIZE)
    phase = positions.astype(F32)[:, None] * frequency[None, :]
    cosine, sine = jnp.cos(phase), jnp.sin(phase)
    cosine = jnp.concatenate([cosine, cosine], axis=1)
    sine = jnp.concatenate([-sine, sine], axis=1)
    pos_col, pos_row = positions[:, None], positions[None, :]

    own_experts = (
        jnp.arange(E, dtype=jnp.int32)[None, :]
        == ((c ^ jnp.arange(C, dtype=jnp.int32)) * S + s)[:, None]
    ).astype(BF16)
    hit = dot(own_experts, hits_column, 1, 1).reshape(C, S, T)
    slot = (jnp.cumsum(hit, axis=2) - hit).astype(jnp.int32)
    target = jnp.where(
        hit > 0.5, jnp.arange(S, dtype=jnp.int32)[None, :, None] * cap + slot, -E * cap
    )
    *picks, place = plan(target.reshape(C, M), rows)

    h1 = norm_rows(x_parts, gain_attn.reshape(1, D))
    qkv = dot(h1, w_qkv, 1, 0)
    mix, totals = attend_forward(qkv, hc, head_gains, cosine, sine, pos_col, pos_row)
    mixes = gather_ctx(mix)
    mix_t = turn_mixes(mixes)
    attn_cols = out_proj(mixes, w_out_cols, c_vec).reshape(C, T, dc)
    attn_out = exchange_ctx([attn_cols[d] for d in range(C)])
    r1, h2 = residual(x_own, attn_out, gain_moe.reshape(1, D), c_vec)

    h2_column = gather_shard(h2)

    def dispatch(v):
        sent = [None] * C
        for d in [C - 1] + list(range(1, C - 1)) + [0]:
            sent[d] = dot(picks[d], v, 1, 0).astype(BF16)
        return exchange_ctx(sent)

    cot_in = dispatch(cot_column)
    expert_in = dispatch(h2_column)

    wg, wu, wd = expert_gate[0], expert_up[0], expert_down[0]
    me_vec = me.astype(jnp.int32).reshape(1)
    back_extra = round_up(2 * E, LANES)
    done = [None] * C
    for d in [0] + list(range(C - 1, 0, -1)):
        done[d] = expert_piece(
            expert_in[d], cot_in[d], router_wide, wg, wu, wd, me_vec, E, back_extra
        )
    mixed_rows, back_rows, hidden, d_expert_out, d_gate, d_up = (list(v) for v in zip(*done))
    back_in = exchange_ctx(back_rows)
    back_sum = sum_shard(combine(place, back_in, 0, D + back_extra, 768))
    mixed_in = exchange_ctx(mixed_rows)
    grad_gate, grad_up, grad_down = expert_grads(expert_in, d_gate, d_up, hidden, d_expert_out)

    d_r1, d_attn_own, grad_router, grad_norm_moe = turn_back(
        back_sum, r1, h2, out_cot[0], hits_wide, router_wide, gain_moe.reshape(1, D), E
    )
    d_attn_parts = gather_ctx(d_attn_own)
    grad_out_piece = sum_shard(out_grads(mix_t, d_attn_parts, c_vec))
    d_attn = jnp.concatenate(d_attn_parts, axis=0)
    d_mix = dot(d_attn, w_out_rows, 1, 1).astype(BF16)
    d_q, d_kv, gain_grads = attend_backward(
        qkv, d_mix, mix, totals, hc, head_gains, cosine, sine, pos_col, pos_row
    )
    d_qkv = jnp.concatenate([d_q, d_kv], axis=1)

    x_seq = jnp.concatenate(x_parts, axis=0).astype(F32)
    d_h1_partial = dot(d_qkv, w_qkv, 1, 1)
    grad_norm_attn = jnp.sum(d_h1_partial * (x_seq * inverse_rms(x_seq)), axis=0)

    def shard_column(v):
        return jnp.pad(v.reshape(S, gs), ((0, 0), (0, ws - gs))).reshape(-1)

    wide = round_up(E + 4, LANES)
    lane = jnp.arange(wide, dtype=jnp.int32)[None, :]
    small = jnp.pad(grad_router[:, :E], ((0, 0), (0, wide - E)))
    columns = (
        grad_norm_attn,
        grad_norm_moe.reshape(D),
        shard_column(gain_grads[0]),
        shard_column(gain_grads[1]),
    )
    for i, v in enumerate(columns):
        small = small + jnp.where(lane == E + i, v[:, None], 0.0)
    owned_partial = weight_grads(h1, d_q, d_kv, small.astype(BF16))
    owned = sum_shard(owned_partial)

    d_h1_parts = d_h1_partial.astype(BF16).reshape(C, T, D)
    d_h1_in = exchange_ctx([d_h1_parts[d] for d in range(C)])
    grad_in = input_back(x_own, d_h1_in, d_r1, gain_attn.reshape(1, D))[None]

    halves = [sum_shard(combine(place, mixed_in, i * D // 2, (i + 1) * D // 2)) for i in range(2)]
    mixture = jnp.concatenate(halves, axis=1).astype(F32)
    block_out = (r1 + mixture).astype(BF16)[None]

    out_parts = gather_ctx(grad_out_piece)
    owned_parts = gather_ctx(owned)
    grad_query, grad_key, grad_value, mine = assemble(owned_parts, c_vec, qc, share)
    grad_out = assemble_columns(out_parts, c_vec)
    return (
        block_out,
        grad_in,
        grad_query,
        grad_key,
        grad_value,
        grad_out,
        mine[:, :E],
        mine[:, E],
        mine[:, E + 1],
        mine[:gs, E + 2],
        mine[:gs, E + 3],
        grad_gate[None],
        grad_up[None],
        grad_down[None],
    )


def solution(mesh):
    token = P("shard", "ctx", None)
    row = P("shard", None)
    vector = P("shard")
    expert = P(("ctx", "shard"), None, None)
    return jax.shard_map(
        layer,
        mesh=mesh,
        in_specs=(token, token, token, P())
        + (vector,) * 4
        + (row,) * 5
        + (expert,) * 3,
        out_specs=(token, token) + (row,) * 5 + (vector,) * 4 + (expert,) * 3,
        check_vma=False,
    )
```

```python
import math

import jax
import jax.numpy as jnp
from jax import lax
from jax.experimental import pallas as pl
from jax.experimental.pallas import tpu as pltpu
from jax.sharding import PartitionSpec as P


QUERY_HEADS = 32
KEY_VALUE_HEADS = 4
HEAD_SIZE = 128
TOP = 8

EPS = 1e-06
THETA = 1000000.0
MASKED = -1e30
LANES = 128
VMEM_LIMIT = 58 * 1024 * 1024
F32 = jnp.float32
BF16 = jnp.bfloat16


def dot(a, b, ca=1, cb=0):
    return lax.dot_general(a, b, (((ca,), (cb,)), ((), ())), preferred_element_type=F32)


def params(**kw):
    return pltpu.CompilerParams(vmem_limit_bytes=VMEM_LIMIT, **kw)


def inverse_rms(v):
    return lax.rsqrt(jnp.mean(v * v, axis=-1, keepdims=True) + EPS)


def turn(v, cosine, sine):
    return v * cosine + pltpu.roll(v, HEAD_SIZE // 2, 1) * sine


def head(pre, gain, cosine, sine):
    return turn(pre * inverse_rms(pre) * gain, cosine, sine).astype(BF16)


def head_back(grad, pre, gain, cosine, sine):
    g = turn(grad, cosine, -sine)
    r = inverse_rms(pre)
    n = pre * r
    scaled = g * gain
    back = r * (scaled - n * jnp.mean(n * scaled, axis=-1, keepdims=True))
    return back.astype(BF16), jnp.sum(g * n, axis=0, keepdims=True)


def attend_forward(qkv, heads, gains, cosine, sine, pos_col, pos_row):
    n = qkv.shape[0]
    hs = HEAD_SIZE
    factor = math.log2(math.e) / math.sqrt(HEAD_SIZE)

    def kernel(q_ref, k_ref, v_ref, gain_ref, cos_ref, sin_ref, pc_ref, pr_ref, out_ref, tot_ref, key_s, val_s, bias_s):
        h = pl.program_id(0)

        @pl.when(h == 0)
        def _():
            key_s[...] = head(k_ref[...], gain_ref[1:2, :], cos_ref[...], sin_ref[...])
            val_s[:, :hs] = v_ref[...].astype(BF16)
            val_s[:, hs:] = jnp.ones((n, hs), BF16)
            bias_s[...] = jnp.where(pc_ref[...] >= pr_ref[...], 0.0, MASKED)
            tot_ref[...] = jnp.zeros_like(tot_ref)

        q = head(q_ref[...], gain_ref[0:1, :], cos_ref[...], sin_ref[...])
        e = jnp.exp2(dot(q, key_s[...], 1, 1) * factor + bias_s[...]).astype(BF16)
        both = dot(e, val_s[...])
        inverse = 1.0 / both[:, hs:]
        out_ref[...] = (both[:, :hs] * inverse).astype(BF16)
        lane = lax.broadcasted_iota(jnp.int32, (n, hs), 1)
        tot_ref[...] = jnp.where(lane == h, inverse, tot_ref[...])

    full = lambda a: pl.BlockSpec(a.shape, lambda h: (0, 0))
    return pl.pallas_call(
        kernel,
        grid=(heads,),
        in_specs=[
            pl.BlockSpec((n, hs), lambda h: (0, h)),
            pl.BlockSpec((n, hs), lambda h: (0, heads)),
            pl.BlockSpec((n, hs), lambda h: (0, heads + 1)),
            full(gains),
            full(cosine),
            full(sine),
            full(pos_col),
            full(pos_row),
        ],
        out_specs=[pl.BlockSpec((n, hs), lambda h: (0, h)), pl.BlockSpec((n, hs), lambda h: (0, 0))],
        out_shape=[
            jax.ShapeDtypeStruct((n, heads * hs), BF16),
            jax.ShapeDtypeStruct((n, hs), F32),
        ],
        scratch_shapes=[pltpu.VMEM((n, hs), BF16), pltpu.VMEM((n, 2 * hs), BF16), pltpu.VMEM((n, n), F32)],
        compiler_params=params(),
        name="attend",
    )(qkv, qkv, qkv, gains, cosine, sine, pos_col, pos_row)


def attend_backward(qkv, d_mix, mix, totals, heads, gains, cosine, sine, pos_col, pos_row):
    n = qkv.shape[0]
    hs = HEAD_SIZE
    scale = 1.0 / math.sqrt(HEAD_SIZE)
    factor = math.log2(math.e) / math.sqrt(HEAD_SIZE)

    def kernel(q_ref, k_ref, v_ref, dm_ref, mix_ref, tot_ref, gain_ref, cos_ref, sin_ref, pc_ref, pr_ref, dq_ref, dkv_ref, gg_ref, key_s, val_s, dk_s, dv_s, bias_s):
        h = pl.program_id(0)

        @pl.when(h == 0)
        def _():
            key_s[...] = head(k_ref[...], gain_ref[1:2, :], cos_ref[...], sin_ref[...])
            val_s[...] = v_ref[...].astype(BF16)
            bias_s[...] = jnp.where(pc_ref[...] >= pr_ref[...], 0.0, MASKED)
            dk_s[...] = jnp.zeros_like(dk_s)
            dv_s[...] = jnp.zeros_like(dv_s)
            gg_ref[...] = jnp.zeros_like(gg_ref)

        pre = q_ref[...]
        q = head(pre, gain_ref[0:1, :], cos_ref[...], sin_ref[...])
        dm = dm_ref[...]
        lane = lax.broadcasted_iota(jnp.int32, (n, hs), 1)
        inverse = jnp.sum(jnp.where(lane == h, tot_ref[...], 0.0), axis=-1, keepdims=True)
        centre = jnp.sum(dm.astype(F32) * mix_ref[...].astype(F32), axis=-1, keepdims=True)
        p = jnp.exp2(dot(q, key_s[...], 1, 1) * factor + bias_s[...]) * inverse
        dp = dot(dm, val_s[...], 1, 1)
        ds = (p * (dp - centre)).astype(BF16)
        dq = dot(ds, key_s[...]) * scale
        dk_s[...] += dot(ds, q, 0, 0)
        dv_s[...] += dot(p.astype(BF16), dm, 0, 0)
        back, gg = head_back(dq, pre, gain_ref[0:1, :], cos_ref[...], sin_ref[...])
        dq_ref[...] = back
        gg_ref[0:1, :] += gg

        @pl.when(h == heads - 1)
        def _():
            back, gg = head_back(
                dk_s[...] * scale, k_ref[...], gain_ref[1:2, :], cos_ref[...], sin_ref[...]
            )
            dkv_ref[:, :hs] = back
            dkv_ref[:, hs:] = dv_s[...].astype(BF16)
            gg_ref[1:2, :] = gg

    full = lambda a: pl.BlockSpec(a.shape, lambda h: (0, 0))
    col = pl.BlockSpec((n, hs), lambda h: (0, h))
    return pl.pallas_call(
        kernel,
        grid=(heads,),
        in_specs=[
            col,
            pl.BlockSpec((n, hs), lambda h: (0, heads)),
            pl.BlockSpec((n, hs), lambda h: (0, heads + 1)),
            col,
            col,
            full(totals),
            full(gains),
            full(cosine),
            full(sine),
            full(pos_col),
            full(pos_row),
        ],
        out_specs=[col, pl.BlockSpec((n, 2 * hs), lambda h: (0, 0)), pl.BlockSpec((8, hs), lambda h: (0, 0))],
        out_shape=[
            jax.ShapeDtypeStruct((n, heads * hs), BF16),
            jax.ShapeDtypeStruct((n, 2 * hs), BF16),
            jax.ShapeDtypeStruct((8, hs), F32),
        ],
        scratch_shapes=[
            pltpu.VMEM((n, hs), BF16),
            pltpu.VMEM((n, hs), BF16),
            pltpu.VMEM((n, hs), F32),
            pltpu.VMEM((n, hs), F32),
            pltpu.VMEM((n, n), F32),
        ],
        compiler_params=params(),
        name="detend",
    )(qkv, qkv, qkv, d_mix, mix, totals, gains, cosine, sine, pos_col, pos_row)


def expert_piece(x, cot, router, wg, wu, wd, me, experts, back_extra):
    r, d = x.shape
    f = wg.shape[1]
    extra = cot.shape[1] - d

    def kernel(me_ref, x_ref, cot_ref, router_ref, wg_ref, wu_ref, wd_ref,
               mixed_ref, back_ref, hid_ref, deo_ref, dg_ref, du_ref):
        own = me_ref[0]
        xv = x_ref[...]
        lane = lax.broadcasted_iota(jnp.int32, (r, extra), 1)
        mask = (cot_ref[:, d:].astype(F32) > 0.5) & (lane < experts)
        kept = jnp.where(mask, dot(xv, router_ref[...]), MASKED)
        e = jnp.where(mask, jnp.exp(kept - jnp.max(kept, axis=-1, keepdims=True)), 0.0)
        total = jnp.sum(e, axis=-1, keepdims=True)
        gate = jnp.sum(jnp.where(lane == own, e, 0.0), axis=-1, keepdims=True) / jnp.where(total > 0.0, total, 1.0)
        gp = dot(xv, wg_ref[...])
        up = dot(xv, wu_ref[...])
        sig = jax.nn.sigmoid(gp)
        silu = gp * sig
        hid = (silu * up).astype(BF16)
        hid_ref[...] = hid
        eo = dot(hid, wd_ref[...]).astype(BF16).astype(F32)
        dout = cot_ref[:, :d].astype(F32)
        dgr = jnp.sum(dout * eo, axis=-1, keepdims=True)
        mixed_ref[...] = (gate * eo).astype(BF16)
        deo = (gate * dout).astype(BF16)
        deo_ref[...] = deo
        dh = dot(deo, wd_ref[...], 1, 1)
        dg = (dh * up * sig * (1.0 + gp * (1.0 - sig))).astype(BF16)
        du = (dh * silu).astype(BF16)
        dg_ref[...] = dg
        du_ref[...] = du
        back_ref[:, :d] = (dot(dg, wg_ref[...], 1, 1) + dot(du, wu_ref[...], 1, 1)).astype(BF16)
        lane = lax.broadcasted_iota(jnp.int32, (r, back_extra), 1)
        high = dgr.astype(BF16).astype(F32)
        low = dgr - high
        back_ref[:, d:] = jnp.where(lane == own, high, jnp.where(lane == own + experts, low, 0.0)).astype(BF16)

    vm = pl.BlockSpec(memory_space=pltpu.VMEM)
    return pl.pallas_call(
        kernel,
        in_specs=[pl.BlockSpec(memory_space=pltpu.SMEM)] + [vm] * 6,
        out_specs=[vm] * 6,
        out_shape=[
            jax.ShapeDtypeStruct((r, d), BF16),
            jax.ShapeDtypeStruct((r, d + back_extra), BF16),
            jax.ShapeDtypeStruct((r, f), BF16),
            jax.ShapeDtypeStruct((r, d), BF16),
            jax.ShapeDtypeStruct((r, f), BF16),
            jax.ShapeDtypeStruct((r, f), BF16),
        ],
        compiler_params=params(),
        name="piece",
    )(me, x, cot, router, wg, wu, wd)


def expert_grads(xs, dgs, dus, hids, deos, block=256):
    n = len(xs)
    r, d = xs[0].shape
    f = dgs[0].shape[1]

    def kernel(*refs):
        x, dg, du, hid, deo = (refs[i * n : (i + 1) * n] for i in range(5))
        gg_ref, gu_ref, gd_ref, x_s, deo_s, dg_s, du_s, hid_s = refs[5 * n :]

        @pl.when(pl.program_id(0) == 0)
        def _():
            for i in range(n):
                dg_s[i * r : (i + 1) * r, :] = dg[i][...]
                du_s[i * r : (i + 1) * r, :] = du[i][...]
                x_s[i * r : (i + 1) * r, :] = hid[i][:, :block]
            for j in range(f // block):
                if j:
                    for i in range(n):
                        x_s[i * r : (i + 1) * r, :] = hid[i][:, j * block : (j + 1) * block]
                hid_s[j * block : (j + 1) * block, :] = x_s[...].T

        for i in range(n):
            x_s[i * r : (i + 1) * r, :] = x[i][...]
            deo_s[i * r : (i + 1) * r, :] = deo[i][...]
        xt = x_s[...].T
        gg_ref[...] = dot(xt, dg_s[...])
        gu_ref[...] = dot(xt, du_s[...])
        gd_ref[...] = dot(hid_s[...], deo_s[...])

    part = pl.BlockSpec((r, block), lambda j: (0, j))
    whole = pl.BlockSpec((r, f), lambda j: (0, 0))
    return pl.pallas_call(
        kernel,
        grid=(d // block,),
        in_specs=[part] * n + [whole] * (3 * n) + [part] * n,
        out_specs=[pl.BlockSpec((block, f), lambda j: (j, 0))] * 2
        + [pl.BlockSpec((f, block), lambda j: (0, j))],
        out_shape=[jax.ShapeDtypeStruct((d, f), F32)] * 2
        + [jax.ShapeDtypeStruct((f, d), F32)],
        scratch_shapes=[
            pltpu.VMEM((n * r, block), BF16),
            pltpu.VMEM((n * r, block), BF16),
            pltpu.VMEM((n * r, f), BF16),
            pltpu.VMEM((n * r, f), BF16),
            pltpu.VMEM((f, n * r), BF16),
        ],
        compiler_params=params(),
        name="exgrads",
    )(*xs, *dgs, *dus, *hids, *deos)


def combine(place, parts, lo, hi, block=512):
    n = len(parts)
    m = place.shape[0]
    r = parts[0].shape[0]
    first = lo // block

    def kernel(place_ref, *refs):
        v, out_ref, v_s = refs[:n], refs[n], refs[n + 1]
        for i in range(n):
            v_s[i * r : (i + 1) * r, :] = v[i][...]
        out_ref[...] = dot(place_ref[...], v_s[...]).astype(BF16)

    return pl.pallas_call(
        kernel,
        grid=(pl.cdiv(hi - lo, block),),
        in_specs=[pl.BlockSpec(place.shape, lambda j: (0, 0))]
        + [pl.BlockSpec((r, block), lambda j: (0, first + j))] * n,
        out_specs=pl.BlockSpec((m, block), lambda j: (0, j)),
        out_shape=jax.ShapeDtypeStruct((m, hi - lo), BF16),
        scratch_shapes=[pltpu.VMEM((n * r, block), BF16)],
        compiler_params=params(),
    )(place, *parts)


def assemble(parts, c, qc, share):
    n = len(parts)
    rows = parts[0].shape[0]
    hs = HEAD_SIZE
    kw = n // share * hs

    def kernel(c_ref, *refs):
        v = refs[:n]
        q_ref, k_ref, v_ref, small_ref = refs[n:]
        small_ref[...] = sum(v[d][:, qc + 2 * hs :].astype(F32) for d in range(n))
        if share > 1:
            k_ref[...] = jnp.zeros_like(k_ref)
            v_ref[...] = jnp.zeros_like(v_ref)
        for d in range(n):
            at = c_ref[0] ^ d
            q_ref[:, pl.ds(pl.multiple_of(at * qc, qc), qc)] = v[d][:, :qc].astype(F32)
            to = pl.ds(pl.multiple_of(at // share * hs, hs), hs)
            key = v[d][:, qc : qc + hs].astype(F32)
            val = v[d][:, qc + hs : qc + 2 * hs].astype(F32)
            if share > 1:
                k_ref[:, to] += key
                v_ref[:, to] += val
            else:
                k_ref[:, to] = key
                v_ref[:, to] = val

    vm = pl.BlockSpec(memory_space=pltpu.VMEM)
    return pl.pallas_call(
        kernel,
        in_specs=[pl.BlockSpec(memory_space=pltpu.SMEM)] + [vm] * n,
        out_specs=[vm] * 4,
        out_shape=[
            jax.ShapeDtypeStruct((rows, n * qc), F32),
            jax.ShapeDtypeStruct((rows, kw), F32),
            jax.ShapeDtypeStruct((rows, kw), F32),
            jax.ShapeDtypeStruct((rows, parts[0].shape[1] - qc - 2 * hs), F32),
        ],
        compiler_params=params(),
        name="assemble",
    )(c, *parts)


def weight_grads(h1, d_q, d_kv, small, block=256):
    n, d = h1.shape
    qc, kc, sc = d_q.shape[1], d_kv.shape[1], small.shape[1]

    def kernel(h_ref, q_ref, kv_ref, small_ref, out_ref):
        h = h_ref[...].T
        out_ref[:, :qc] = dot(h, q_ref[...], 1, 0).astype(BF16)
        out_ref[:, qc : qc + kc] = dot(h, kv_ref[...], 1, 0).astype(BF16)
        out_ref[:, qc + kc :] = small_ref[...]

    return pl.pallas_call(
        kernel,
        grid=(d // block,),
        in_specs=[
            pl.BlockSpec((n, block), lambda j: (0, j)),
            pl.BlockSpec((n, qc), lambda j: (0, 0)),
            pl.BlockSpec((n, kc), lambda j: (0, 0)),
            pl.BlockSpec((block, sc), lambda j: (j, 0)),
        ],
        out_specs=pl.BlockSpec((block, qc + kc + sc), lambda j: (j, 0)),
        out_shape=jax.ShapeDtypeStruct((d, qc + kc + sc), BF16),
        compiler_params=params(),
        name="wgrads",
    )(h1, d_q, d_kv, small)


def assemble_columns(parts, c):
    n = len(parts)
    rows, w = parts[0].shape

    def kernel(c_ref, *refs):
        for d in range(n):
            at = pl.multiple_of((c_ref[0] ^ d) * w, w)
            refs[n][:, pl.ds(at, w)] = refs[d][...].astype(F32)

    vm = pl.BlockSpec(memory_space=pltpu.VMEM)
    return pl.pallas_call(
        kernel,
        in_specs=[pl.BlockSpec(memory_space=pltpu.SMEM)] + [vm] * n,
        out_specs=vm,
        out_shape=jax.ShapeDtypeStruct((rows, n * w), F32),
        compiler_params=params(),
        name="columns",
    )(c, *parts)


def gather_rows(picks, pieces, block=768):
    n, k = len(picks), len(pieces)
    rows, m = picks[0].shape
    t, d = pieces[0].shape

    def kernel(*refs):
        pick, piece, out, v_s = refs[:n], refs[n : n + k], refs[n + k : -1], refs[-1]
        for j in range(k):
            v_s[j * t : (j + 1) * t, :] = piece[j][...]
        for i in range(n):
            out[i][...] = dot(pick[i][...], v_s[...]).astype(BF16)

    return pl.pallas_call(
        kernel,
        grid=(pl.cdiv(d, block),),
        in_specs=[pl.BlockSpec((rows, m), lambda j: (0, 0))] * n
        + [pl.BlockSpec((t, block), lambda j: (0, j))] * k,
        out_specs=[pl.BlockSpec((rows, block), lambda j: (0, j))] * n,
        out_shape=[jax.ShapeDtypeStruct((rows, d), BF16)] * n,
        scratch_shapes=[pltpu.VMEM((m, block), BF16)],
        compiler_params=params(),
        name="grab",
    )(*picks, *pieces)


def pack(w_query, w_key, w_value, at, qc):
    ws = w_query.shape[0]
    hs = HEAD_SIZE

    def kernel(at_ref, q_ref, k_ref, v_ref, out_ref):
        out_ref[:, :qc] = q_ref[...]
        out_ref[:, qc : qc + hs] = k_ref[...]
        out_ref[:, qc + hs :] = v_ref[...]

    head_spec = pl.BlockSpec((ws, hs), lambda j, at_ref: (0, at_ref[1]))
    return pl.pallas_call(
        kernel,
        grid_spec=pltpu.PrefetchScalarGridSpec(
            num_scalar_prefetch=1,
            grid=(1,),
            in_specs=[
                pl.BlockSpec((ws, qc), lambda j, at_ref: (0, at_ref[0])),
                head_spec,
                head_spec,
            ],
            out_specs=pl.BlockSpec((ws, qc + 2 * hs), lambda j, at_ref: (0, 0)),
        ),
        out_shape=jax.ShapeDtypeStruct((ws, qc + 2 * hs), BF16),
        compiler_params=params(),
        name="pack",
    )(at, w_query, w_key, w_value)


def plan(targets, rows, placed, block=LANES):
    n, m = targets.shape

    def kernel(row_ref, col_ref, *outs):
        ids = lax.broadcasted_iota(jnp.int32, (rows, block), 0)
        for d in range(n):
            outs[d][...] = jnp.where(row_ref[d : d + 1, :] == ids, 1.0, 0.0).astype(BF16)
        if not placed:
            return
        ids = lax.broadcasted_iota(jnp.int32, (block, n * rows), 1)
        hot = col_ref[:, 0:1] == ids
        for d in range(1, n):
            hot = hot | (col_ref[:, d : d + 1] + d * rows == ids)
        outs[n][...] = jnp.where(hot, 1.0, 0.0).astype(BF16)

    return pl.pallas_call(
        kernel,
        grid=(m // block,),
        in_specs=[
            pl.BlockSpec((n, block), lambda j: (0, j)),
            pl.BlockSpec((block, n), lambda j: (j, 0)),
        ],
        out_specs=[pl.BlockSpec((rows, block), lambda j: (0, j))] * n
        + [pl.BlockSpec((block, n * rows), lambda j: (j, 0))] * placed,
        out_shape=[jax.ShapeDtypeStruct((rows, m), BF16)] * n
        + [jax.ShapeDtypeStruct((m, n * rows), BF16)] * placed,
        compiler_params=params(),
    )(targets, targets.T)


def norm_rows(parts, gain):
    n = len(parts)
    t, d = parts[0].shape

    def kernel(gain_ref, *refs):
        for i in range(n):
            v = refs[i][...].astype(F32)
            refs[n][i * t : (i + 1) * t, :] = (v * inverse_rms(v) * gain_ref[...]).astype(BF16)

    vm = pl.BlockSpec(memory_space=pltpu.VMEM)
    return pl.pallas_call(
        kernel,
        in_specs=[vm] * (n + 1),
        out_specs=vm,
        out_shape=jax.ShapeDtypeStruct((n * t, d), BF16),
        compiler_params=params(),
        name="norm_rows",
    )(gain, *parts)


def out_proj(parts, w_cols, c):
    n = len(parts)
    t, k = parts[0].shape
    w = w_cols.shape[1]

    def kernel(c_ref, *refs):
        w_ref, out_ref, acc_ref = refs[n:]
        d = pl.program_id(0)
        for i in range(n):

            @pl.when(d == i)
            def _():
                part = dot(refs[i][...], w_ref[...])
                for b in range(n):
                    to, of = b * (t // n), (b ^ i) * (t // n)
                    block = part[of : of + t // n, :]
                    if i == 0:
                        acc_ref[to : to + t // n, :] = block
                    elif i < n - 1:
                        acc_ref[to : to + t // n, :] += block
                    else:
                        total = acc_ref[to : to + t // n, :] + block
                        out_ref[to : to + t // n, :] = total.astype(BF16)

    return pl.pallas_call(
        kernel,
        grid_spec=pltpu.PrefetchScalarGridSpec(
            num_scalar_prefetch=1,
            grid=(n,),
            in_specs=[pl.BlockSpec((t, k), lambda d, c_ref: (0, 0))] * n
            + [pl.BlockSpec((k, w), lambda d, c_ref: (c_ref[0] ^ d, 0))],
            out_specs=pl.BlockSpec((t, w), lambda d, c_ref: (0, 0)),
            scratch_shapes=[pltpu.VMEM((t, w), F32)],
        ),
        out_shape=jax.ShapeDtypeStruct((t, w), BF16),
        compiler_params=params(),
        name="oproj",
    )(c, *parts, w_cols)


def turn_mixes(mixes, block=512):
    n = len(mixes)
    t, k = mixes[0].shape
    nb = k // block

    def kernel(*refs):
        i = pl.program_id(0)
        for e in range(n):

            @pl.when(i == e)
            def _():
                refs[n][...] = refs[e][...].T

    def pick(e):
        return pl.BlockSpec((t, block), lambda i, j: (0, jnp.where(i < e, 0, jnp.where(i > e, nb - 1, j))))

    return pl.pallas_call(
        kernel,
        grid=(n, nb),
        in_specs=[pick(e) for e in range(n)],
        out_specs=pl.BlockSpec((block, t), lambda i, j: (i * nb + j, 0)),
        out_shape=jax.ShapeDtypeStruct((n * k, t), BF16),
        compiler_params=params(),
        name="turn",
    )(*mixes)


def out_grads(mix_t, d_parts, c, block=512):
    n = len(d_parts)
    k, t = mix_t.shape[0] // n, mix_t.shape[1]
    rows, d_model = d_parts[0].shape
    w = d_model // n
    nb = k // block

    def kernel(c_ref, m_ref, *refs):
        dp, out_ref, d_s = refs[:n], refs[n], refs[n + 1]
        i, j = pl.program_id(0), pl.program_id(1)

        @pl.when((i == 0) & (j == 0))
        def _():
            for e in range(n):
                for b in range(n):
                    d_s[e, b * rows : (b + 1) * rows, :] = dp[b ^ e][...]

        out_ref[...] = dot(m_ref[...], d_s[i]).astype(BF16)

    return pl.pallas_call(
        kernel,
        grid_spec=pltpu.PrefetchScalarGridSpec(
            num_scalar_prefetch=1,
            grid=(n, nb),
            in_specs=[pl.BlockSpec((block, t), lambda i, j, c_ref: (i * nb + j, 0))]
            + [pl.BlockSpec((rows, w), lambda i, j, c_ref: (0, c_ref[0]))] * n,
            out_specs=pl.BlockSpec((block, w), lambda i, j, c_ref: ((c_ref[0] ^ i) * nb + j, 0)),
            scratch_shapes=[pltpu.VMEM((n, t, w), BF16)],
        ),
        out_shape=jax.ShapeDtypeStruct((n * k, w), BF16),
        compiler_params=params(),
        name="out_grads",
    )(c, mix_t, *d_parts)


def residual(x, parts, gain, c):
    n = len(parts)
    w = parts[0].shape[1]

    def kernel(c_ref, x_ref, gain_ref, *refs):
        r1_ref, h2_ref = refs[n:]
        for i in range(n):
            at = pl.ds(pl.multiple_of((c_ref[0] ^ i) * w, w), w)
            r1_ref[:, at] = x_ref[:, at].astype(F32) + refs[i][...].astype(F32)
        v = r1_ref[...]
        h2_ref[...] = (v * inverse_rms(v) * gain_ref[...]).astype(BF16)

    vm = pl.BlockSpec(memory_space=pltpu.VMEM)
    return pl.pallas_call(
        kernel,
        in_specs=[pl.BlockSpec(memory_space=pltpu.SMEM)] + [vm] * (n + 2),
        out_specs=[vm] * 2,
        out_shape=[jax.ShapeDtypeStruct(x.shape, F32), jax.ShapeDtypeStruct(x.shape, BF16)],
        compiler_params=params(),
        name="resid",
    )(c, x, gain, *parts)


def masked_softmax(logits, mask):
    kept = jnp.where(mask, logits, MASKED)
    e = jnp.where(mask, jnp.exp(kept - jnp.max(kept, axis=-1, keepdims=True)), 0.0)
    total = jnp.sum(e, axis=-1, keepdims=True)
    return e / jnp.where(total > 0.0, total, 1.0)


def norm_back(v, gain, grad):
    r = inverse_rms(v)
    n = v * r
    scaled = grad * gain
    back = r * (scaled - n * jnp.mean(n * scaled, axis=-1, keepdims=True))
    return back, grad * n


def turn_back(back_sum, r1, h2, cot, hits, router, gain, experts):
    t, d = r1.shape
    extra = hits.shape[1]

    def kernel(back_ref, r1_ref, h2_ref, cot_ref, hit_ref, router_ref, gain_ref, dr_ref, da_ref, gr_ref, gn_ref):
        gates = masked_softmax(
            dot(h2_ref[...], router_ref[...]), hit_ref[...].astype(F32) > 0.5
        )
        high = back_ref[:, d : d + extra].astype(F32)
        if experts % LANES:
            d_gates = high + pltpu.roll(high, extra - experts, 1)
        else:
            d_gates = high + back_ref[:, d + experts : d + experts + extra].astype(F32)
        centre = jnp.sum(gates * d_gates, axis=-1, keepdims=True)
        d_logits = (gates * (d_gates - centre)).astype(BF16)
        gr_ref[...] = dot(h2_ref[...], d_logits, 0, 0)
        d_h2 = back_ref[:, :d].astype(F32) + dot(d_logits, router_ref[...], 1, 1)
        back, gain_rows = norm_back(r1_ref[...], gain_ref[...], d_h2)
        gn_ref[...] = jnp.sum(gain_rows, axis=0, keepdims=True)
        total = cot_ref[...].astype(F32) + back
        dr_ref[...] = total
        da_ref[...] = total.astype(BF16)

    vm = pl.BlockSpec(memory_space=pltpu.VMEM)
    return pl.pallas_call(
        kernel,
        in_specs=[vm] * 7,
        out_specs=[vm] * 4,
        out_shape=[
            jax.ShapeDtypeStruct((t, d), F32),
            jax.ShapeDtypeStruct((t, d), BF16),
            jax.ShapeDtypeStruct((d, extra), F32),
            jax.ShapeDtypeStruct((1, d), F32),
        ],
        compiler_params=params(),
        name="tback",
    )(back_sum, r1, h2, cot, hits, router, gain)


def input_back(x, parts, d_r1, gain):
    n = len(parts)

    def kernel(x_ref, dr_ref, gain_ref, *refs):
        grad = refs[0][...].astype(F32)
        for i in range(1, n):
            grad = grad + refs[i][...].astype(F32)
        back, _ = norm_back(x_ref[...].astype(F32), gain_ref[...], grad)
        refs[n][...] = dr_ref[...] + back

    vm = pl.BlockSpec(memory_space=pltpu.VMEM)
    return pl.pallas_call(
        kernel,
        in_specs=[vm] * (n + 3),
        out_specs=vm,
        out_shape=jax.ShapeDtypeStruct(x.shape, F32),
        compiler_params=params(),
        name="inback",
    )(x, d_r1, gain, *parts)


def round_up(n, m):
    return (n + m - 1) // m * m


def rows_of_pair(pair_value, row_count, pair_count):
    row_ids = jnp.arange(row_count, dtype=jnp.int32)
    half = row_count // 2
    block = jnp.where(row_ids >= half, 2 * pair_count - 1 - pair_value, pair_value)
    return block * half + row_ids % half


def layer(
    hidden_in,
    out_cot,
    routes,
    block_pairs,
    norm_attn,
    norm_moe,
    q_gain,
    k_gain,
    w_query,
    w_key,
    w_value,
    w_out,
    w_router,
    expert_gate,
    expert_up,
    expert_down,
):
    C = lax.axis_size("ctx")
    S = lax.axis_size("shard")
    T = hidden_in.shape[1]
    D = hidden_in.shape[2]
    E = C * S
    M = S * T
    QW = QUERY_HEADS * HEAD_SIZE
    qc = QW // C
    share = C // KEY_VALUE_HEADS
    hc = qc // HEAD_SIZE
    cap = max(2, (17 * T * TOP + 16 * E - 1) // (16 * E))
    rows = S * cap
    ws = w_query.shape[0]
    gs = q_gain.shape[0]
    po = QW // E
    c = lax.axis_index("ctx")
    s = lax.axis_index("shard")
    me = c * S + s
    c_vec = c.astype(jnp.int32).reshape(1)

    def exchange_ctx(parts):
        out = [parts[0]]
        for d in range(1, C):
            out.append(lax.ppermute(parts[d], "ctx", [(i, i ^ d) for i in range(C)]))
        return out

    def gather_ctx(v):
        return exchange_ctx([v] * C)

    def gather_shard(v):
        return lax.all_gather(v, "shard", axis=0, tiled=True)

    def sum_shard(v):
        return lax.psum_scatter(v, "shard", scatter_dimension=0, tiled=True)

    at = jnp.stack([c, c // share]).astype(jnp.int32)
    packed = pack(w_query, w_key, w_value, at, qc)
    w_qkv = gather_shard(packed)
    hits = (
        (routes[0][:, :, None] == jnp.arange(E, dtype=jnp.int32)[None, None, :])
        .any(axis=1)
        .astype(BF16)
    )
    rw = ws * E // T
    nw = ws // T
    small_parts = [
        hits,
        w_router.reshape(T, rw),
        norm_moe.reshape(T, nw),
        norm_attn.reshape(T, nw),
        jnp.pad(jnp.concatenate([q_gain, k_gain]), (0, T - 2 * gs)).reshape(T, 1),
    ]
    small_width = round_up(E + rw + 2 * nw + 1, LANES)
    small_parts.append(jnp.zeros((T, small_width - E - rw - 2 * nw - 1), BF16))
    table = gather_shard(jnp.concatenate(small_parts, axis=1))
    x_own = hidden_in[0]
    x_parts = gather_ctx(x_own)
    hits_column = table[:, :E]
    router = table[:, E : E + rw].reshape(D, E)
    gain_moe = table[:, E + rw : E + rw + nw].reshape(D).astype(F32)
    gain_attn = table[:, E + rw + nw : E + rw + 2 * nw].reshape(D).astype(F32)
    head_gains = table[:, E + rw + 2 * nw].reshape(S, T).astype(F32)
    head_gains = jnp.concatenate(
        [
            head_gains[:, :gs].reshape(1, -1),
            head_gains[:, gs : 2 * gs].reshape(1, -1),
            jnp.zeros((6, HEAD_SIZE), F32),
        ],
        axis=0,
    )

    pieces = []
    for i in range(C):
        pairs = [(p // S * S + p // C, p) for p in range(E) if p % C == i]
        pieces.append(lax.ppermute(w_out[i * po : (i + 1) * po], ("ctx", "shard"), pairs))
    piece = sum(pieces[1:], pieces[0])
    w_out_rows = gather_shard(piece)
    dc = D // C
    w_out_cols = gather_shard(lax.dynamic_slice_in_dim(w_out, c * dc, dc, 1))

    extra = round_up(E, LANES)
    hits_wide = jnp.pad(hits, ((0, 0), (0, extra - E)))
    cot_own = jnp.concatenate([out_cot[0], hits_wide], axis=1)

    def hop_shard(v, d):
        return lax.ppermute(v, "shard", [(i, i ^ d) for i in range(S)])

    far = [cot_own] + [hop_shard(cot_own, d) for d in range(2, S, 2)]
    near = [hop_shard(v, 1) for v in far]
    cot_pieces = [v for both in zip(far, near) for v in both]
    router_wide = jnp.pad(router, ((0, 0), (0, extra - E)))

    pairs_here = jnp.stack([block_pairs[c ^ d] for d in range(C)])
    positions = jax.vmap(lambda p: rows_of_pair(p, T, C))(pairs_here).reshape(-1)
    frequency = THETA ** (-(jnp.arange(HEAD_SIZE // 2, dtype=F32) * 2.0) / HEAD_SIZE)
    phase = positions.astype(F32)[:, None] * frequency[None, :]
    cosine, sine = jnp.cos(phase), jnp.sin(phase)
    cosine = jnp.concatenate([cosine, cosine], axis=1)
    sine = jnp.concatenate([-sine, sine], axis=1)
    pos_col, pos_row = positions[:, None], positions[None, :]

    own_experts = (
        jnp.arange(E, dtype=jnp.int32)[None, :]
        == ((c ^ jnp.arange(C, dtype=jnp.int32)) * S + s)[:, None]
    ).astype(BF16)
    hit = dot(own_experts, hits_column, 1, 1).reshape(C, S, T)
    slot = (jnp.cumsum(hit, axis=2) - hit).astype(jnp.int32)
    target = jnp.where(
        hit > 0.5, jnp.arange(S, dtype=jnp.int32)[None, :, None] * cap + slot, -E * cap
    )
    *picks, place = plan(target.reshape(C, M), rows, 1)
    near_target = [lax.dynamic_index_in_dim(target, s ^ j, 1, False) for j in range(S)]
    near_picks = plan(jnp.concatenate(near_target, axis=1), rows, 0)

    h1 = norm_rows(x_parts, gain_attn.reshape(1, D))
    qkv = dot(h1, w_qkv, 1, 0)
    mix, totals = attend_forward(qkv, hc, head_gains, cosine, sine, pos_col, pos_row)
    mixes = gather_ctx(mix)
    mix_t = turn_mixes(mixes)
    attn_cols = out_proj(mixes, w_out_cols, c_vec).reshape(C, T, dc)
    attn_out = exchange_ctx([attn_cols[d] for d in range(C)])
    r1, h2 = residual(x_own, attn_out, gain_moe.reshape(1, D), c_vec)

    h2_column = gather_shard(h2)

    cot_rows = [None] * C
    for d in list(range(C - 1, -1, -1)):
        cot_rows[d] = gather_rows([near_picks[d]], cot_pieces)[0]
    cot_in = exchange_ctx(cot_rows)
    h2_rows = [None] * C
    for d in [C - 1] + list(range(1, C - 1)) + [0]:
        h2_rows[d] = dot(picks[d], h2_column, 1, 0).astype(BF16)
    expert_in = exchange_ctx(h2_rows)

    wg, wu, wd = expert_gate[0], expert_up[0], expert_down[0]
    me_vec = me.astype(jnp.int32).reshape(1)
    back_extra = round_up(2 * E, LANES)
    done = [None] * C
    for d in [0] + list(range(C - 1, 0, -1)):
        done[d] = expert_piece(
            expert_in[d], cot_in[d], router_wide, wg, wu, wd, me_vec, E, back_extra
        )
    mixed_rows, back_rows, hidden, d_expert_out, d_gate, d_up = (list(v) for v in zip(*done))
    back_in = exchange_ctx(back_rows)
    back_sum = sum_shard(combine(place, back_in, 0, D + back_extra, 768))
    mixed_in = exchange_ctx(mixed_rows)
    grad_gate, grad_up, grad_down = expert_grads(expert_in, d_gate, d_up, hidden, d_expert_out)

    d_r1, d_attn_own, grad_router, grad_norm_moe = turn_back(
        back_sum, r1, h2, out_cot[0], hits_wide, router_wide, gain_moe.reshape(1, D), E
    )
    d_attn_parts = gather_ctx(d_attn_own)
    grad_out_piece = sum_shard(out_grads(mix_t, d_attn_parts, c_vec))
    d_attn = jnp.concatenate(d_attn_parts, axis=0)
    d_mix = dot(d_attn, w_out_rows, 1, 1).astype(BF16)
    d_q, d_kv, gain_grads = attend_backward(
        qkv, d_mix, mix, totals, hc, head_gains, cosine, sine, pos_col, pos_row
    )
    d_qkv = jnp.concatenate([d_q, d_kv], axis=1)

    x_seq = jnp.concatenate(x_parts, axis=0).astype(F32)
    d_h1_partial = dot(d_qkv, w_qkv, 1, 1)
    grad_norm_attn = jnp.sum(d_h1_partial * (x_seq * inverse_rms(x_seq)), axis=0)

    def shard_column(v):
        return jnp.pad(v.reshape(S, gs), ((0, 0), (0, ws - gs))).reshape(-1)

    wide = round_up(E + 4, LANES)
    lane = jnp.arange(wide, dtype=jnp.int32)[None, :]
    small = jnp.pad(grad_router[:, :E], ((0, 0), (0, wide - E)))
    columns = (
        grad_norm_attn,
        grad_norm_moe.reshape(D),
        shard_column(gain_grads[0]),
        shard_column(gain_grads[1]),
    )
    for i, v in enumerate(columns):
        small = small + jnp.where(lane == E + i, v[:, None], 0.0)
    owned_partial = weight_grads(h1, d_q, d_kv, small.astype(BF16))
    owned = sum_shard(owned_partial)

    d_h1_parts = d_h1_partial.astype(BF16).reshape(C, T, D)
    d_h1_in = exchange_ctx([d_h1_parts[d] for d in range(C)])
    grad_in = input_back(x_own, d_h1_in, d_r1, gain_attn.reshape(1, D))[None]

    halves = [sum_shard(combine(place, mixed_in, i * D // 2, (i + 1) * D // 2)) for i in range(2)]
    mixture = jnp.concatenate(halves, axis=1).astype(F32)
    block_out = (r1 + mixture).astype(BF16)[None]

    out_parts = gather_ctx(grad_out_piece)
    owned_parts = gather_ctx(owned)
    grad_query, grad_key, grad_value, mine = assemble(owned_parts, c_vec, qc, share)
    grad_out = assemble_columns(out_parts, c_vec)
    return (
        block_out,
        grad_in,
        grad_query,
        grad_key,
        grad_value,
        grad_out,
        mine[:, :E],
        mine[:, E],
        mine[:, E + 1],
        mine[:gs, E + 2],
        mine[:gs, E + 3],
        grad_gate[None],
        grad_up[None],
        grad_down[None],
    )


def solution(mesh):
    token = P("shard", "ctx", None)
    row = P("shard", None)
    vector = P("shard")
    expert = P(("ctx", "shard"), None, None)
    return jax.shard_map(
        layer,
        mesh=mesh,
        in_specs=(token, token, token, P())
        + (vector,) * 4
        + (row,) * 5
        + (expert,) * 3,
        out_specs=(token, token) + (row,) * 5 + (vector,) * 4 + (expert,) * 3,
        check_vma=False,
    )
```
